256 devices in a mesh: gz: 64 (over x, y, z_lo), gy: 4 (over z_hi, core).
Axes of the slice: x: 4, y: 4, z: 8 (z_hi: 2, z_lo: 4; z = z_hi * 4 + z_lo), core: 2. Of those that a mesh axis runs over, the one named last changes fastest.
Arguments:
- potential: float32 [192, 512, 2048], P('gz', 'gy'), may hold values from -3 to 301
- external: float32 [192, 512, 2048], P('gz', 'gy'), may hold values from -4 to 4
Outputs:
- dual_field: float32 [192, 512, 2048], P('gz', 'gy')
- density_log: float32 [192, 512, 2048], P('gz', 'gy')
The draws below stay inside these ranges and needn't reach their ends.
All inputs are finite; a program needn't handle non-finite values.
Results may differ from the reference program's by a relative error of at most 0.0001.
Values sent between devices are 32-bit elements; how exact they have to be, the bound alone decides.
A program may use at most 128 MiB of HBM per device.

```python
import jax
import jax.numpy as jnp
from jax import lax

NX = 2048
CY = 128
RADIUS = 128
NY = 512
NZ = 192
N_GY = 4


def draw_potential(key, part):
    field_shape = (NZ, NY, NX)
    exponent_tail = jnp.minimum(jax.random.exponential(key, field_shape, jnp.float32), 18.0)
    rough_part = 3.0 * exponent_tail - 3.0
    return rough_part


def levels(stream_key, shape, cuts, low, top_value):
    factor_of = 1.0
    for axis_at, parts in cuts:
        steps = jax.random.uniform(jax.random.fold_in(jax.random.fold_in(stream_key, 6), axis_at), (parts,), jnp.float32, low / len(cuts), top_value / len(cuts))
        factor_of = factor_of * jnp.repeat(jnp.exp(steps), shape[axis_at] // parts).reshape((-1,) + (1,) * (len(shape) - 1 - axis_at))
    return factor_of


def noise(key, extent, width, limit, cuts=(), held_as=jnp.bfloat16):
    level = levels(key, extent, cuts, -0.22, 0.18) if cuts else 1.0
    values = jax.random.normal(key, extent, jnp.float32) * width * level
    return jnp.minimum(jnp.maximum(values, -limit), limit).astype(held_as)


def setup_inputs(seed: int = 0) -> dict:
    arg_keys = jax.random.split(jax.random.key(seed), 3)
    potential = draw_potential(jax.random.fold_in(arg_keys[2], 71), 0)
    external = noise(arg_keys[1], (NZ, NY, NX), 1.0, 4.0, ((0, 64), (1, 4)), jnp.float32)
    return {"potential": potential, "external": external}


HIGHEST = lax.Precision.HIGHEST


def log_kernel(row_count, col_count, offset, radius):
    in_index = lax.broadcasted_iota(jnp.int32, (row_count, col_count), 0)
    out_index = lax.broadcasted_iota(jnp.int32, (row_count, col_count), 1)
    apart = in_index - offset - out_index
    distance = apart.astype(jnp.float32)
    inside = jnp.abs(apart) <= radius
    return jnp.where(inside, jnp.exp(-2.0 * distance * distance / float(radius * radius)), 0.0)


def along_last(source, radius):
    leading = source.shape[:-1]
    length = source.shape[-1]
    block_size = 2 * radius
    block_count = length // block_size
    border = jnp.full(leading + (radius,), -jnp.inf, jnp.float32)
    padded = jnp.concatenate([border, source, border], axis=-1)
    pieces = padded.reshape(leading + (block_count + 1, block_size))
    window = jnp.concatenate([pieces[..., :-1, :], pieces[..., 1:, :]], axis=-1)
    highest_value = jnp.max(window, axis=-1, keepdims=True)
    weights = jnp.exp(window - highest_value)
    kernel_table = log_kernel(2 * block_size, block_size, radius, radius)
    summed = jnp.einsum("...w,wo->...o", weights, kernel_table, precision=HIGHEST)
    return (jnp.log(summed) + highest_value).reshape(leading + (length,))


def along_middle(extended, own_rows, radius):
    highest_value = jnp.max(extended, axis=1, keepdims=True)
    weights = jnp.exp(extended - highest_value)
    kernel_table = log_kernel(own_rows + 2 * radius, own_rows, radius, radius)
    summed = jnp.einsum("zwx,wo->zox", weights, kernel_table, precision=HIGHEST)
    return jnp.log(summed) + highest_value


def along_first(source, radius):
    length = source.shape[0]
    highest_value = jnp.max(source, axis=0, keepdims=True)
    weights = jnp.exp(source - highest_value)
    kernel_table = log_kernel(length, length, 0, radius)
    summed = jnp.einsum("wyx,wo->oyx", weights, kernel_table, precision=HIGHEST)
    return jnp.log(summed) + highest_value


def proximal(logs, outer_field):
    shifted = logs - 0.5 * outer_field
    softer = jnp.maximum(shifted, 0.0) + jnp.log1p(jnp.exp(-jnp.abs(shifted)))
    log_level = jnp.log1p(softer)
    for newton_step in range(2):
        exp_level = jnp.exp(log_level)
        log_level = log_level - (log_level + exp_level - shifted) / (1.0 + exp_level)
    return log_level - logs, log_level


def reference(potential, external):
    depth = RADIUS

    def plane_pass(plane):
        along_x = along_last(plane, depth)
        border = jnp.full((depth, NX), -jnp.inf, jnp.float32)
        padded = jnp.concatenate([border, along_x, border], axis=0)
        results = []
        for block_index in range(N_GY):
            window = lax.slice_in_dim(padded, block_index * CY, block_index * CY + CY + 2 * depth, axis=0)
            results.append(along_middle(window[None], CY, depth)[0])
        return jnp.concatenate(results, axis=0)

    along_y = lax.map(plane_pass, potential)

    def column_block(block_index, carry):
        dual_part, density_part = carry
        start = (block_index * CY).astype(jnp.int32)
        logs = lax.dynamic_slice_in_dim(along_y, start, CY, axis=1)
        outer_field = lax.dynamic_slice_in_dim(external, start, CY, axis=1)
        new_dual, new_density = proximal(along_first(logs, depth), outer_field)
        return (lax.dynamic_update_slice_in_dim(dual_part, new_dual, start, axis=1),
                lax.dynamic_update_slice_in_dim(density_part, new_density, start, axis=1))

    zero_field = jnp.zeros((NZ, NY, NX), jnp.float32)
    dual_field, density_log = lax.fori_loop(0, NY // CY, column_block, (zero_field, zero_field))
    return dual_field, density_log
```

```python
import jax
import jax.numpy as jnp
from jax import lax
from jax.experimental import pallas as pl
from jax.experimental.pallas import tpu as pltpu
from jax.sharding import PartitionSpec as P

RADIUS = 128
LANES = 128
ROWS = 8
WIDE = 256


def log_kernel(row_count, col_count, offset, radius):
    in_index = lax.broadcasted_iota(jnp.int32, (row_count, col_count), 0)
    out_index = lax.broadcasted_iota(jnp.int32, (row_count, col_count), 1)
    apart = in_index - offset - out_index
    distance = apart.astype(jnp.float32)
    inside = jnp.abs(apart) <= radius
    return jnp.where(inside, jnp.exp(-2.0 * distance * distance / float(radius * radius)), 0.0)


def halves(values):
    high = values.astype(jnp.bfloat16)
    low = (values - high.astype(jnp.float32)).astype(jnp.bfloat16)
    return high, low


def table_halves(table):
    high = lax.reduce_precision(table, 8, 7)
    return high.astype(jnp.bfloat16), (table - high).astype(jnp.bfloat16)


def table_rows(table):
    high, low = table_halves(table)
    return jnp.concatenate([high, high, low], axis=0)


def table_cols(table):
    high, low = table_halves(table)
    return jnp.concatenate([high, high, low], axis=1)


def dot(left, right):
    return jnp.dot(left, right, preferred_element_type=jnp.float32)


def x_kernel(source, table, out):
    blocks = source.shape[-1] // LANES
    for r in range(source.shape[0]):
        peaks, weights = [], []
        for k in range(blocks):
            cells = source[r, :, k * LANES:(k + 1) * LANES]
            peak = jnp.max(cells, axis=1, keepdims=True)
            peaks.append(peak)
            weights.append(jnp.exp(cells - peak))
        for k in range(blocks // 2):
            near = [j for j in range(2 * k - 1, 2 * k + 3) if 0 <= j < blocks]
            top = peaks[near[0]]
            for j in near[1:]:
                top = jnp.maximum(top, peaks[j])
            window = jnp.concatenate([weights[j] * jnp.exp(peaks[j] - top) for j in near], axis=1)
            high, low = halves(window)
            start = (near[0] - (2 * k - 1)) * LANES
            width = len(near) * LANES
            size = 4 * LANES
            tall = [table[i * size + start:i * size + start + width, :] for i in range(3)]
            summed = dot(high, tall[0]) + dot(low, tall[1]) + dot(high, tall[2])
            logs = jnp.log(summed) + top
            turned = logs.T
            out[k * (WIDE // ROWS):(k + 1) * (WIDE // ROWS), r * ROWS:(r + 1) * ROWS, :] = turned.reshape(
                WIDE // ROWS, ROWS, LANES
            )


def yz_kernel(source, y_table, z_table, out, middle):
    groups, parts, rows, _ = source.shape
    depth = groups * rows // ROWS
    batch = 8
    size = 3 * LANES

    @pl.loop(0, groups // batch)
    def _(step):
        first = step * batch
        peaks, weights = [], []
        for b in range(parts):
            cells = source[pl.ds(first, batch), b].reshape(batch * rows, LANES)
            peak = jnp.max(cells, axis=1, keepdims=True)
            peaks.append(peak)
            weights.append(jnp.exp(cells - peak))
        for b in range(parts):
            near = [j for j in range(b - 1, b + 2) if 0 <= j < parts]
            top = peaks[near[0]]
            for j in near[1:]:
                top = jnp.maximum(top, peaks[j])
            window = jnp.concatenate([weights[j] * jnp.exp(peaks[j] - top) for j in near], axis=1)
            high, low = halves(window)
            start = (near[0] - (b - 1)) * LANES
            width = len(near) * LANES
            tall = [y_table[i * size + start:i * size + start + width, :] for i in range(3)]
            summed = dot(high, tall[0]) + dot(low, tall[1]) + dot(high, tall[2])
            at = pl.multiple_of(first * rows, batch * rows)
            middle[b, pl.ds(at, batch * rows), :] = jnp.log(summed) + top

    for b in range(parts):
        tops = jnp.max(middle[b].reshape(depth, ROWS, LANES), axis=0)
        for x in range(ROWS):
            cells = middle[b, pl.ds(x, depth, stride=ROWS), :]
            top = tops[x:x + 1, :]
            weights = jnp.exp(cells - top)
            high, low = halves(weights)
            summed = dot(z_table[...], jnp.concatenate([high, low, high], axis=0))
            middle[b, pl.ds(x, depth, stride=ROWS), :] = jnp.log(summed) + top
        out[:, b] = middle[b].reshape(groups, rows, LANES)


def proximal(logs, outer_field):
    shifted = logs - 0.5 * outer_field
    softer = jnp.maximum(shifted, 0.0) + jnp.log1p(jnp.exp(-jnp.abs(shifted)))
    log_level = jnp.log1p(softer)
    for newton_step in range(2):
        exp_level = jnp.exp(log_level)
        log_level = log_level - (log_level + exp_level - shifted) / (1.0 + exp_level)
    return log_level - logs, log_level


def end_kernel(source, outer, dual, density):
    blocks = outer.shape[-1] // WIDE
    per = WIDE // ROWS
    for r in range(outer.shape[0]):
        for k in range(blocks):
            turned = source[k * per:(k + 1) * per, r * ROWS:(r + 1) * ROWS, :].reshape(WIDE, LANES)
            at = slice(k * WIDE, (k + 1) * WIDE)
            dual_part, density_part = proximal(turned.T, outer[r, :, at])
            dual[r, :, at] = dual_part
            density[r, :, at] = density_part


PARAMS = pltpu.CompilerParams(vmem_limit_bytes=56 << 20)


def local(potential, external):
    depth, own_rows, length = potential.shape
    groups, parts = lax.axis_size("gz"), lax.axis_size("gy")
    devices = groups * parts
    rows = depth * ROWS
    vmem = pl.BlockSpec(memory_space=pltpu.VMEM)
    x_table = table_rows(log_kernel(4 * LANES, WIDE, RADIUS, RADIUS))
    y_table = table_rows(log_kernel(3 * LANES, LANES, RADIUS, RADIUS))
    z_table = table_cols(log_kernel(groups * depth, groups * depth, 0, RADIUS))
    tiles = jax.ShapeDtypeStruct((devices, rows, LANES), jnp.float32)
    along_x = pl.pallas_call(
        x_kernel, out_shape=tiles, in_specs=[vmem, vmem], out_specs=vmem, compiler_params=PARAMS, name="along_x"
    )(potential, x_table)
    received = lax.all_to_all(along_x, ("gz", "gy"), 0, 0, tiled=True)
    along_z = pl.pallas_call(
        yz_kernel,
        out_shape=jax.ShapeDtypeStruct((groups, parts, rows, LANES), jnp.float32),
        in_specs=[vmem] * 3,
        out_specs=vmem,
        scratch_shapes=[pltpu.VMEM((parts, groups * rows, LANES), jnp.float32)],
        compiler_params=PARAMS,
        name="along_yz",
    )(received.reshape(groups, parts, rows, LANES), y_table, z_table)
    returned = lax.all_to_all(along_z.reshape(devices, rows, LANES), ("gz", "gy"), 0, 0, tiled=True)
    field = jax.ShapeDtypeStruct(potential.shape, jnp.float32)
    return pl.pallas_call(
        end_kernel, out_shape=(field, field), in_specs=[vmem] * 2, out_specs=(vmem, vmem), compiler_params=PARAMS, name="proximal"
    )(returned, external)


def solution(mesh):
    return jax.shard_map(
        local,
        mesh=mesh,
        in_specs=(P("gz", "gy", None), P("gz", "gy", None)),
        out_specs=(P("gz", "gy", None), P("gz", "gy", None)),
        check_vma=False,
    )
```

```python
import jax
import jax.numpy as jnp
from jax import lax
from jax.experimental import pallas as pl
from jax.experimental.pallas import tpu as pltpu
from jax.sharding import PartitionSpec as P

RADIUS = 128
LANES = 128
ROWS = 8
WIDE = 256


def log_kernel(row_count, col_count, offset, radius):
    in_index = lax.broadcasted_iota(jnp.int32, (row_count, col_count), 0)
    out_index = lax.broadcasted_iota(jnp.int32, (row_count, col_count), 1)
    apart = in_index - offset - out_index
    distance = apart.astype(jnp.float32)
    inside = jnp.abs(apart) <= radius
    return jnp.where(inside, jnp.exp(-2.0 * distance * distance / float(radius * radius)), 0.0)


def halves(values):
    high = values.astype(jnp.bfloat16)
    low = (values - high.astype(jnp.float32)).astype(jnp.bfloat16)
    return high, low


def table_halves(table):
    high = lax.reduce_precision(table, 8, 7)
    return high.astype(jnp.bfloat16), (table - high).astype(jnp.bfloat16)


def table_rows(table):
    high, low = table_halves(table)
    return jnp.concatenate([high, high, low], axis=0)


def table_cols(table):
    high, low = table_halves(table)
    return jnp.concatenate([high, high, low], axis=1)


def dot(left, right):
    return jnp.dot(left, right, preferred_element_type=jnp.float32)


MESH = pl.DeviceIdType.MESH
CHUNKS = 4
RING = 16
GROUPS = 4
EMPTY = -1e30


def chain_kernel(potential, x_table, y_table, z_table, home, cells, a, b, c, d, e, f, load_sem, send_sem, recv_sem, own_sem):
    depth, own_rows, length = potential.shape
    slab, part = lax.axis_index("gz"), lax.axis_index("gy")
    spot, lane = slab // GROUPS, slab % GROUPS
    core = part % 2
    level = (part // 2) * 4 + lane
    sign = 1 - 2 * core
    step_x = length // CHUNKS
    tile = a.shape[2]

    load = pltpu.make_async_copy(potential, cells.at[:, :, pl.ds(LANES, length)], load_sem)
    load.start()

    def z_peer(s):
        t = (s * 3) % RING
        to_level = (level + sign * (t % 8) + 8) % 8
        to_core = (core + t // 8) % 2
        return spot * GROUPS + to_level % 4, (to_level // 4) * 2 + to_core

    def xy_peer(s):
        t = (s * 5) % RING
        to_x = (spot // 4 + sign * (t % 4) + 4) % 4
        to_y = (spot % 4 + sign * (t // 4) + 4) % 4
        return to_x * 4 + to_y

    barrier = pltpu.get_barrier_semaphore()

    @pl.loop(1, RING)
    def _(s):
        pl.semaphore_signal(barrier, inc=1, device_id=z_peer(s), device_id_type=MESH)
        pl.semaphore_signal(barrier, inc=1, device_id=(xy_peer(s) * GROUPS + lane, part), device_id_type=MESH)

    def order(slab_of, part_of):
        return ((part_of // 2) * 4 + slab_of % GROUPS) * 2 + part_of % 2

    mine = order(slab, part)
    slot = lane * GROUPS + part

    def send(source, target, stage, chunk, device):
        pltpu.make_async_remote_copy(
            src_ref=source,
            dst_ref=target,
            send_sem=send_sem.at[stage, chunk],
            recv_sem=recv_sem.at[stage, chunk],
            device_id=device,
            device_id_type=MESH,
        ).start()

    def keep(source, target, stage, chunk):
        return pltpu.make_async_copy(source, target, own_sem.at[stage, chunk])

    def x_stage(chunk):
        @pl.loop(0, depth)
        def _(r):
            peaks, weights = [], []
            for k in range(6):
                at = pl.multiple_of(chunk * step_x + k * LANES, LANES)
                block = cells[r, :, pl.ds(at, LANES)]
                peak = jnp.max(block, axis=1, keepdims=True)
                peaks.append(peak)
                weights.append(jnp.exp(block - peak))
            size = 4 * LANES
            for k in range(2):
                near = range(2 * k, 2 * k + 4)
                top = peaks[near[0]]
                for j in near[1:]:
                    top = jnp.maximum(top, peaks[j])
                window = jnp.concatenate([weights[j] * jnp.exp(peaks[j] - top) for j in near], axis=1)
                high, low = halves(window)
                summed = (
                    dot(high, x_table[:size, :]) + dot(low, x_table[size:2 * size, :]) + dot(high, x_table[2 * size:, :])
                )
                turned = (jnp.log(summed) + top).T
                a[chunk, 8 * k:8 * k + 8, pl.ds(pl.multiple_of(r * 32, 32), 32), :] = turned.reshape(8, 32, LANES)

        return None

    def x_send(chunk):
        keep(a.at[chunk, mine], b.at[chunk, slot], 0, chunk).start()

        @pl.loop(1, RING)
        def _(s):
            to = z_peer(s)
            send(a.at[chunk, order(*to)], b.at[chunk, slot], 0, chunk, to)

    def arrive(stage, chunk, source, target):
        view = pltpu.make_async_remote_copy(
            src_ref=source,
            dst_ref=target,
            send_sem=send_sem.at[stage, chunk],
            recv_sem=recv_sem.at[stage, chunk],
            device_id=(slab, part),
            device_id_type=MESH,
        )
        return view

    def y_stage(chunk):
        keep(a.at[chunk, mine], b.at[chunk, slot], 0, chunk).wait()
        arrive(0, chunk, a.at[chunk, pl.ds(0, RING - 1)], b.at[chunk, pl.ds(0, RING - 1)]).wait_recv()
        size = 3 * LANES

        @pl.loop(0, GROUPS)
        def _(lo):
            peaks, weights = [], []
            for k in range(GROUPS):
                block = b[chunk, lo * GROUPS + k]
                peak = jnp.max(block, axis=1, keepdims=True)
                peaks.append(peak)
                weights.append(jnp.exp(block - peak))
            for k in range(GROUPS):
                near = [j for j in range(k - 1, k + 2) if 0 <= j < GROUPS]
                top = peaks[near[0]]
                for j in near[1:]:
                    top = jnp.maximum(top, peaks[j])
                window = jnp.concatenate([weights[j] * jnp.exp(peaks[j] - top) for j in near], axis=1)
                high, low = halves(window)
                start = (near[0] - (k - 1)) * LANES
                width = len(near) * LANES
                tall = [y_table[i * size + start:i * size + start + width, :] for i in range(3)]
                logs = jnp.log(dot(high, tall[0]) + dot(low, tall[1]) + dot(high, tall[2])) + top
                for r in range(depth):
                    for g in range(4):
                        at = pl.multiple_of((lo * depth + r) * ROWS, ROWS)
                        first = (r * 4 + g) * ROWS
                        c[chunk, k * 4 + g, pl.ds(at, ROWS), :] = logs[first:first + ROWS, :]

        rows = pl.ds(pl.multiple_of(spot * tile, tile), tile)
        keep(c.at[chunk, spot], d.at[chunk, rows], 1, chunk).start()

        @pl.loop(1, RING)
        def _(s):
            to = xy_peer(s)
            send(c.at[chunk, to], d.at[chunk, rows], 1, chunk, (to * GROUPS + lane, part))

    def z_stage(chunk):
        rows = pl.ds(pl.multiple_of(spot * tile, tile), tile)
        keep(c.at[chunk, spot], d.at[chunk, rows], 1, chunk).wait()
        arrive(1, chunk, c.at[chunk, pl.ds(0, RING - 1)], d.at[chunk, pl.ds(0, (RING - 1) * tile)]).wait_recv()
        deep = RING * tile // ROWS
        tops = jnp.max(d[chunk].reshape(deep, ROWS, LANES), axis=0)
        for x in range(0, ROWS, 2):
            top = jnp.concatenate([tops[x:x + 1, :], tops[x + 1:x + 2, :]], axis=1)
            pair = jnp.concatenate([d[chunk, pl.ds(x + i, deep, stride=ROWS), :] for i in range(2)], axis=1)
            high, low = halves(jnp.exp(pair - top))
            logs = jnp.log(dot(z_table[...], jnp.concatenate([high, low, high], axis=0))) + top
            for i in range(2):
                e[chunk, pl.ds(x + i, deep, stride=ROWS), :] = logs[:, i * LANES:(i + 1) * LANES]
        keep(e.at[chunk, rows], f.at[chunk, spot], 2, chunk).start()

        @pl.loop(1, RING)
        def _(s):
            to = xy_peer(s)
            there = pl.ds(pl.multiple_of(to * tile, tile), tile)
            send(e.at[chunk, there], f.at[chunk, spot], 2, chunk, (to * GROUPS + lane, part))

    def piece(chunk, slab_of, part_of):
        rows = tile // GROUPS
        at = pl.multiple_of((slab_of % GROUPS) * rows, rows)
        return f.at[chunk, pl.ds(part_of * 4, 4), pl.ds(at, rows)]

    def back_stage(chunk):
        rows = pl.ds(pl.multiple_of(spot * tile, tile), tile)
        keep(e.at[chunk, rows], f.at[chunk, spot], 2, chunk).wait()
        arrive(2, chunk, e.at[chunk, pl.ds(0, (RING - 1) * tile)], f.at[chunk, pl.ds(0, RING - 1)]).wait_recv()
        keep(piece(chunk, slab, part), home.at[chunk, mine], 3, chunk).start()

        @pl.loop(1, RING)
        def _(s):
            to = z_peer(s)
            send(piece(chunk, *to), home.at[chunk, mine], 3, chunk, to)

    edge = jnp.full((depth, own_rows, LANES), EMPTY, jnp.float32)
    cells[:, :, :LANES] = edge
    cells[:, :, LANES + length:] = edge
    load.wait()
    x_stage(0)
    pl.semaphore_wait(barrier, 2 * (RING - 1))
    x_send(0)

    @pl.loop(1, CHUNKS)
    def _(chunk):
        x_stage(chunk)
        x_send(chunk)

    @pl.loop(0, CHUNKS)
    def _(chunk):
        y_stage(chunk)

        @pl.when(chunk > 0)
        def _():
            back_stage(chunk - 1)

        z_stage(chunk)

    back_stage(CHUNKS - 1)

    @pl.loop(0, CHUNKS)
    def _(chunk):
        some = pl.ds(0, RING - 1)
        flat = pl.ds(0, (RING - 1) * tile)
        arrive(0, chunk, a.at[chunk, some], b.at[chunk, some]).wait_send()
        arrive(1, chunk, c.at[chunk, some], d.at[chunk, flat]).wait_send()
        arrive(2, chunk, e.at[chunk, flat], f.at[chunk, some]).wait_send()
        keep(piece(chunk, slab, part), home.at[chunk, mine], 3, chunk).wait()
        last = arrive(3, chunk, home.at[chunk, some], home.at[chunk, some])
        last.wait_send()
        last.wait_recv()


def proximal(logs, outer_field):
    shifted = logs - 0.5 * outer_field
    softer = jnp.maximum(shifted, 0.0) + jnp.log1p(jnp.exp(-jnp.abs(shifted)))
    log_level = jnp.log1p(softer)
    for newton_step in range(2):
        exp_level = jnp.exp(log_level)
        log_level = log_level - (log_level + exp_level - shifted) / (1.0 + exp_level)
    return log_level - logs, log_level


def end_kernel(source, outer, dual, density):
    blocks = outer.shape[-1] // WIDE
    per = WIDE // ROWS
    for k in range(blocks):
        turned = source[k * per:(k + 1) * per].reshape(WIDE, LANES)
        at = slice(k * WIDE, (k + 1) * WIDE)
        dual_part, density_part = proximal(turned.T, outer[0, :, at])
        dual[0, :, at] = dual_part
        density[0, :, at] = density_part


def local(potential, external):
    depth, own_rows, length = potential.shape
    groups = lax.axis_size("gz")
    rows = depth * ROWS
    tile = GROUPS * rows
    vmem = pl.BlockSpec(memory_space=pltpu.VMEM)
    anywhere = pl.BlockSpec(memory_space=pl.ANY)
    x_table = table_rows(log_kernel(4 * LANES, WIDE, RADIUS, RADIUS))
    y_table = table_rows(log_kernel(3 * LANES, LANES, RADIUS, RADIUS))
    z_table = table_cols(log_kernel(groups * depth, groups * depth, 0, RADIUS))
    stack = pltpu.VMEM((CHUNKS, RING, tile, LANES), jnp.float32)
    long = pltpu.VMEM((CHUNKS, RING * tile, LANES), jnp.float32)
    along_z = pl.pallas_call(
        chain_kernel,
        out_shape=jax.ShapeDtypeStruct((CHUNKS, RING, GROUPS, rows, LANES), jnp.float32),
        in_specs=[anywhere, vmem, vmem, vmem],
        out_specs=anywhere,
        scratch_shapes=[
            pltpu.VMEM((depth, own_rows, length + 2 * LANES), jnp.float32),
            stack,
            stack,
            stack,
            long,
            long,
            stack,
            pltpu.SemaphoreType.DMA,
            pltpu.SemaphoreType.DMA((4, CHUNKS)),
            pltpu.SemaphoreType.DMA((4, CHUNKS)),
            pltpu.SemaphoreType.DMA((4, CHUNKS)),
        ],
        compiler_params=pltpu.CompilerParams(collective_id=0, has_side_effects=True, vmem_limit_bytes=48 << 20),
        name="along_xyz",
    )(potential, x_table, y_table, z_table)
    field = jax.ShapeDtypeStruct(potential.shape, jnp.float32)
    wide = length // CHUNKS
    block = pl.BlockSpec((1, own_rows, wide), lambda r, k: (r, 0, k))
    return pl.pallas_call(
        end_kernel,
        grid=(depth, CHUNKS),
        out_shape=(field, field),
        in_specs=[pl.BlockSpec((wide // ROWS, ROWS, LANES), lambda r, k: (k, r, 0)), block],
        out_specs=(block, block),
        name="proximal",
    )(along_z.reshape(length // ROWS, rows, LANES), external)


def solution(mesh):
    return jax.shard_map(
        local,
        mesh=mesh,
        in_specs=(P("gz", "gy", None), P("gz", "gy", None)),
        out_specs=(P("gz", "gy", None), P("gz", "gy", None)),
        check_vma=False,
    )
```

```python
import jax
import jax.numpy as jnp
import numpy as np
from jax import lax
from jax.experimental import pallas as pl
from jax.experimental.pallas import tpu as pltpu
from jax.sharding import PartitionSpec as P

RADIUS = 128
LANES = 128
ROWS = 8
WIDE = 256


def log_kernel(row_count, col_count, offset, radius):
    apart = np.arange(row_count)[:, None] - offset - np.arange(col_count)[None, :]
    distance = apart.astype(np.float32)
    inside = np.abs(apart) <= radius
    return np.where(inside, np.exp(-2.0 * distance * distance / float(radius * radius)), 0.0).astype(np.float32)


def halves(values):
    high = values.astype(jnp.bfloat16)
    low = (values - high.astype(jnp.float32)).astype(jnp.bfloat16)
    return high, low


def table_halves(table):
    high = table.astype(jnp.bfloat16)
    return high, (table - high.astype(np.float32)).astype(jnp.bfloat16)


def table_rows(table):
    return np.concatenate(table_halves(table), axis=0)


def table_cols(table):
    high, low = table_halves(table)
    return np.concatenate([high, high, low], axis=1)


def dot(left, right):
    return jnp.dot(left, right, preferred_element_type=jnp.float32)


def proximal(logs, outer_field):
    shifted = logs - 0.5 * outer_field
    softer = jnp.maximum(shifted, 0.0) + jnp.log(1.0 + jnp.exp(-jnp.abs(shifted)))
    exp_level = 1.0 + softer
    log_level = jnp.log(exp_level)
    log_level = log_level - (log_level + exp_level - shifted) / (1.0 + exp_level)
    exp_level = jnp.exp(log_level)
    log_level = log_level - (log_level + exp_level - shifted) / (1.0 + exp_level)
    return log_level - logs, log_level


def finish(turned, outer, at, r, out_at, dual, density):
    for k in range(at[1] // WIDE):
        there = pl.ds(pl.multiple_of(at[0] + k * WIDE, WIDE), WIDE)
        put = pl.ds(pl.multiple_of(out_at + k * WIDE, WIDE), WIDE)
        dual_part, density_part = proximal(turned(k).T, outer[r, :, there])
        dual[r, :, put] = dual_part
        density[r, :, put] = density_part


def end_kernel(done_dual, done_density, rest, outer, dual, density, rest_in, outer_in, dual_in, density_in, sems):
    depth, own_rows, length = outer.shape
    before = done_dual.shape[-1]
    width = length - before
    late = [
        pltpu.make_async_copy(rest, rest_in, sems.at[0]),
        pltpu.make_async_copy(outer.at[:, :, pl.ds(before, width)], outer_in, sems.at[1]),
    ]
    for copy in late:
        copy.start()
    out = [
        pltpu.make_async_copy(done_dual, dual.at[:, :, pl.ds(0, before)], sems.at[2]),
        pltpu.make_async_copy(done_density, density.at[:, :, pl.ds(0, before)], sems.at[3]),
    ]
    for copy in out:
        copy.start()
    for copy in late:
        copy.wait()
    for r in range(depth):
        def turned(k):
            return rest_in[8 * k:8 * k + 8, :, r * ROWS:(r + 1) * ROWS, :].reshape(WIDE, LANES)

        finish(turned, outer_in, (0, width), r, 0, dual_in, density_in)
        for i, (source, target) in enumerate(((dual_in, dual), (density_in, density))):
            copy = pltpu.make_async_copy(source.at[r], target.at[r, :, pl.ds(before, width)], sems.at[4 + 2 * r + i])
            copy.start()
            out.append(copy)
    for copy in out:
        copy.wait()


MESH = pl.DeviceIdType.MESH
CHUNKS = 4
RING = 16
GROUPS = 4
EMPTY = -1e30


def chain_kernel(
    potential,
    outer,
    x_source,
    y_source,
    z_source,
    done_dual,
    done_density,
    rest,
    cells,
    a,
    b,
    c,
    d,
    e,
    f,
    home,
    outer_in,
    dual_in,
    density_in,
    x_table,
    y_table,
    z_table,
    load_sem,
    send_sem,
    recv_sem,
    own_sem,
    out_sem,
):
    depth, own_rows, length = potential.shape
    slab, part = lax.axis_index("gz"), lax.axis_index("gy")
    spot, lane = slab // GROUPS, slab % GROUPS
    core = part % 2
    level = (part // 2) * 4 + lane
    sign = 1 - 2 * core
    step_x = length // CHUNKS
    tile = a.shape[2]

    early = step_x + LANES
    loads = [
        pltpu.make_async_copy(potential.at[:, :, pl.ds(0, early)], cells.at[:, :, pl.ds(LANES, early)], load_sem.at[0]),
        pltpu.make_async_copy(
            potential.at[:, :, pl.ds(early, length - early)],
            cells.at[:, :, pl.ds(LANES + early, length - early)],
            load_sem.at[1],
        ),
        pltpu.make_async_copy(outer.at[:, :, pl.ds(0, length - step_x)], outer_in, load_sem.at[2]),
    ]
    tables = [
        pltpu.make_async_copy(source, target, load_sem.at[3 + i])
        for i, (source, target) in enumerate(((x_source, x_table), (y_source, y_table), (z_source, z_table)))
    ]
    for load in loads[:1] + tables + loads[1:]:
        load.start()

    def z_peer(s):
        t = (s * 3) % RING
        to_level = (level + sign * (t % 8) + 8) % 8
        to_core = (core + t // 8) % 2
        return spot * GROUPS + to_level % 4, (to_level // 4) * 2 + to_core

    def xy_peer(s):
        t = (s * 5) % RING
        to_x = (spot // 4 + sign * (t % 4) + 4) % 4
        to_y = (spot % 4 + sign * (t // 4) + 4) % 4
        return to_x * 4 + to_y

    barrier = pltpu.get_barrier_semaphore()

    @pl.loop(1, RING)
    def _(s):
        pl.semaphore_signal(barrier, inc=1, device_id=z_peer(s), device_id_type=MESH)
        pl.semaphore_signal(barrier, inc=1, device_id=(xy_peer(s) * GROUPS + lane, part), device_id_type=MESH)

    def order(slab_of, part_of):
        return ((part_of // 2) * 4 + slab_of % GROUPS) * 2 + part_of % 2

    mine = order(slab, part)
    slot = lane * GROUPS + part

    def send(source, target, stage, chunk, device):
        pltpu.make_async_remote_copy(
            src_ref=source,
            dst_ref=target,
            send_sem=send_sem.at[stage, chunk],
            recv_sem=recv_sem.at[stage, chunk],
            device_id=device,
            device_id_type=MESH,
        ).start()

    def keep(source, target, stage, chunk):
        return pltpu.make_async_copy(source, target, own_sem.at[stage, chunk])

    def x_stage(chunk):
        @pl.loop(0, depth)
        def _(r):
            peaks, weights = [], []
            for k in range(6):
                at = pl.multiple_of(chunk * step_x + k * LANES, LANES)
                block = cells[r, :, pl.ds(at, LANES)]
                peak = jnp.max(block, axis=1, keepdims=True)
                peaks.append(peak)
                weights.append(jnp.exp(block - peak))
            size = 4 * LANES
            for k in range(2):
                near = range(2 * k, 2 * k + 4)
                top = peaks[near[0]]
                for j in near[1:]:
                    top = jnp.maximum(top, peaks[j])
                window = jnp.concatenate([weights[j] * jnp.exp(peaks[j] - top) for j in near], axis=1)
                high, low = halves(window)
                summed = (
                    dot(high, x_table[:size, :]) + dot(low, x_table[:size, :]) + dot(high, x_table[size:, :])
                )
                turned = (jnp.log(summed) + top).T
                a[chunk, 8 * k:8 * k + 8, pl.ds(pl.multiple_of(r * 32, 32), 32), :] = turned.reshape(8, 32, LANES)

        return None

    def x_send(chunk):
        keep(a.at[chunk, mine], b.at[chunk, slot], 0, chunk).start()

        @pl.loop(1, RING)
        def _(s):
            to = z_peer(s)
            send(a.at[chunk, order(*to)], b.at[chunk, slot], 0, chunk, to)

    def arrive(stage, chunk, source, target):
        view = pltpu.make_async_remote_copy(
            src_ref=source,
            dst_ref=target,
            send_sem=send_sem.at[stage, chunk],
            recv_sem=recv_sem.at[stage, chunk],
            device_id=(slab, part),
            device_id_type=MESH,
        )
        return view

    def y_stage(chunk):
        keep(a.at[chunk, mine], b.at[chunk, slot], 0, chunk).wait()
        arrive(0, chunk, a.at[chunk, pl.ds(0, RING - 1)], b.at[chunk, pl.ds(0, RING - 1)]).wait_recv()
        size = 3 * LANES

        @pl.loop(0, GROUPS)
        def _(lo):
            peaks, weights = [], []
            for k in range(GROUPS):
                block = b[chunk, lo * GROUPS + k]
                peak = jnp.max(block, axis=1, keepdims=True)
                peaks.append(peak)
                weights.append(jnp.exp(block - peak))
            for k in range(GROUPS):
                near = [j for j in range(k - 1, k + 2) if 0 <= j < GROUPS]
                top = peaks[near[0]]
                for j in near[1:]:
                    top = jnp.maximum(top, peaks[j])
                window = jnp.concatenate([weights[j] * jnp.exp(peaks[j] - top) for j in near], axis=1)
                high, low = halves(window)
                start = (near[0] - (k - 1)) * LANES
                width = len(near) * LANES
                tall = [y_table[i * size + start:i * size + start + width, :] for i in range(2)]
                logs = jnp.log(dot(high, tall[0]) + dot(low, tall[0]) + dot(high, tall[1])) + top
                for r in range(depth):
                    for g in range(4):
                        at = pl.multiple_of((lo * depth + r) * ROWS, ROWS)
                        first = (r * 4 + g) * ROWS
                        c[chunk, k * 4 + g, pl.ds(at, ROWS), :] = logs[first:first + ROWS, :]

        rows = pl.ds(pl.multiple_of(spot * tile, tile), tile)
        keep(c.at[chunk, spot], d.at[chunk, rows], 1, chunk).start()

        @pl.loop(1, RING)
        def _(s):
            to = xy_peer(s)
            send(c.at[chunk, to], d.at[chunk, rows], 1, chunk, (to * GROUPS + lane, part))

    def z_stage(chunk):
        rows = pl.ds(pl.multiple_of(spot * tile, tile), tile)
        keep(c.at[chunk, spot], d.at[chunk, rows], 1, chunk).wait()
        arrive(1, chunk, c.at[chunk, pl.ds(0, RING - 1)], d.at[chunk, pl.ds(0, (RING - 1) * tile)]).wait_recv()
        deep = RING * tile // ROWS
        tops = jnp.max(d[chunk].reshape(deep, ROWS, LANES), axis=0)
        for x in range(0, ROWS, 2):
            top = jnp.concatenate([tops[x:x + 1, :], tops[x + 1:x + 2, :]], axis=1)
            pair = jnp.concatenate([d[chunk, pl.ds(x + i, deep, stride=ROWS), :] for i in range(2)], axis=1)
            high, low = halves(jnp.exp(pair - top))
            logs = jnp.log(dot(z_table[...], jnp.concatenate([high, low, high], axis=0))) + top
            for i in range(2):
                e[chunk, pl.ds(x + i, deep, stride=ROWS), :] = logs[:, i * LANES:(i + 1) * LANES]
        keep(e.at[chunk, rows], f.at[chunk, spot], 2, chunk).start()

        @pl.loop(1, RING)
        def _(s):
            to = xy_peer(s)
            there = pl.ds(pl.multiple_of(to * tile, tile), tile)
            send(e.at[chunk, there], f.at[chunk, spot], 2, chunk, (to * GROUPS + lane, part))

    def piece(chunk, slab_of, part_of):
        rows = tile // GROUPS
        at = pl.multiple_of((slab_of % GROUPS) * rows, rows)
        return f.at[chunk, pl.ds(part_of * 4, 4), pl.ds(at, rows)]

    def back_stage(chunk, place):
        rows = pl.ds(pl.multiple_of(spot * tile, tile), tile)
        keep(e.at[chunk, rows], f.at[chunk, spot], 2, chunk).wait()
        arrive(2, chunk, e.at[chunk, pl.ds(0, (RING - 1) * tile)], f.at[chunk, pl.ds(0, RING - 1)]).wait_recv()
        keep(piece(chunk, slab, part), place.at[mine], 3, chunk).start()

        @pl.loop(1, RING)
        def _(s):
            to = z_peer(s)
            send(piece(chunk, *to), place.at[mine], 3, chunk, to)

    edge = jnp.full((depth, own_rows, LANES), EMPTY, jnp.float32)
    cells[:, :, :LANES] = edge
    cells[:, :, LANES + length:] = edge
    loads[0].wait()
    tables[0].wait()
    x_stage(0)
    pl.semaphore_wait(barrier, 2 * (RING - 1))
    x_send(0)
    for load in loads[1:2] + tables[1:]:
        load.wait()

    @pl.loop(1, CHUNKS)
    def _(chunk):
        x_stage(chunk)
        x_send(chunk)

    @pl.loop(0, CHUNKS)
    def _(chunk):
        y_stage(chunk)

        @pl.when(chunk > 0)
        def _():
            back_stage(chunk - 1, home.at[chunk - 1])

        z_stage(chunk)

    back_stage(CHUNKS - 1, rest)
    loads[2].wait()
    some = pl.ds(0, RING - 1)

    def out_copies(chunk):
        at = pl.ds(pl.multiple_of(chunk * step_x, step_x), step_x)
        return [
            pltpu.make_async_copy(source.at[:, :, at], target.at[:, :, at], out_sem.at[i, chunk])
            for i, (source, target) in enumerate(((dual_in, done_dual), (density_in, done_density)))
        ]

    @pl.loop(0, CHUNKS - 1)
    def _(chunk):
        keep(piece(chunk, slab, part), home.at[chunk, mine], 3, chunk).wait()
        arrive(3, chunk, home.at[chunk, some], home.at[chunk, some]).wait_recv()

        @pl.loop(0, depth)
        def _(r):
            def turned(k):
                rows = pl.ds(pl.multiple_of(r * ROWS, ROWS), ROWS)
                return home[chunk, 8 * k:8 * k + 8, :, rows, :].reshape(WIDE, LANES)

            finish(turned, outer_in, (chunk * step_x, step_x), r, chunk * step_x, dual_in, density_in)

        for copy in out_copies(chunk):
            copy.start()

    @pl.loop(0, CHUNKS - 1)
    def _(chunk):
        for copy in out_copies(chunk):
            copy.wait()

    @pl.loop(0, CHUNKS)
    def _(chunk):
        flat = pl.ds(0, (RING - 1) * tile)
        arrive(0, chunk, a.at[chunk, some], b.at[chunk, some]).wait_send()
        arrive(1, chunk, c.at[chunk, some], d.at[chunk, flat]).wait_send()
        arrive(2, chunk, e.at[chunk, flat], f.at[chunk, some]).wait_send()
        arrive(3, chunk, rest.at[some], rest.at[some]).wait_send()

    keep(piece(CHUNKS - 1, slab, part), rest.at[mine], 3, CHUNKS - 1).wait()
    arrive(3, CHUNKS - 1, rest.at[some], rest.at[some]).wait_recv()


def local(potential, external):
    depth, own_rows, length = potential.shape
    groups = lax.axis_size("gz")
    rows = depth * ROWS
    tile = GROUPS * rows
    wide = length // CHUNKS
    before = length - wide
    anywhere = pl.BlockSpec(memory_space=pl.ANY)
    x_table = jnp.asarray(table_rows(log_kernel(4 * LANES, WIDE, RADIUS, RADIUS)))
    y_table = jnp.asarray(table_rows(log_kernel(3 * LANES, LANES, RADIUS, RADIUS)))
    z_table = jnp.asarray(table_cols(log_kernel(groups * depth, groups * depth, 0, RADIUS)))
    stack = pltpu.VMEM((CHUNKS, RING, tile, LANES), jnp.float32)
    long = pltpu.VMEM((CHUNKS, RING * tile, LANES), jnp.float32)
    done = (depth, own_rows, before)
    done_shape = jax.ShapeDtypeStruct(done, jnp.float32)
    piece = (RING, GROUPS, rows, LANES)
    done_dual, done_density, rest = pl.pallas_call(
        chain_kernel,
        out_shape=(done_shape, done_shape, jax.ShapeDtypeStruct(piece, jnp.float32)),
        in_specs=[pl.BlockSpec(memory_space=pltpu.HBM)] * 5,
        out_specs=(anywhere, anywhere, anywhere),
        scratch_shapes=[
            pltpu.VMEM((depth, own_rows, length + 2 * LANES), jnp.float32),
            stack,
            stack,
            stack,
            long,
            long,
            stack,
            pltpu.VMEM((CHUNKS - 1,) + piece, jnp.float32),
            pltpu.VMEM(done, jnp.float32),
            pltpu.VMEM(done, jnp.float32),
            pltpu.VMEM(done, jnp.float32),
            *[pltpu.VMEM(table.shape, table.dtype) for table in (x_table, y_table, z_table)],
            pltpu.SemaphoreType.DMA((6,)),
            pltpu.SemaphoreType.DMA((4, CHUNKS)),
            pltpu.SemaphoreType.DMA((4, CHUNKS)),
            pltpu.SemaphoreType.DMA((4, CHUNKS)),
            pltpu.SemaphoreType.DMA((2, CHUNKS)),
        ],
        compiler_params=pltpu.CompilerParams(collective_id=0, has_side_effects=True, vmem_limit_bytes=44 << 20),
        name="along_xyz",
    )(*[pltpu.with_memory_space_constraint(v, pltpu.HBM) for v in (potential, external, x_table, y_table, z_table)])
    field = jax.ShapeDtypeStruct(potential.shape, jnp.float32)
    late = pltpu.VMEM((depth, own_rows, wide), jnp.float32)
    return pl.pallas_call(
        end_kernel,
        out_shape=(field, field),
        in_specs=[anywhere] * 3 + [pl.BlockSpec(memory_space=pltpu.HBM)],
        out_specs=(anywhere, anywhere),
        scratch_shapes=[pltpu.VMEM(piece, jnp.float32), late, late, late, pltpu.SemaphoreType.DMA((4 + 2 * depth,))],
        compiler_params=pltpu.CompilerParams(vmem_limit_bytes=16 << 20),
        name="proximal",
    )(done_dual, done_density, rest, pltpu.with_memory_space_constraint(external, pltpu.HBM))


def solution(mesh):
    return jax.shard_map(
        local,
        mesh=mesh,
        in_specs=(P("gz", "gy", None), P("gz", "gy", None)),
        out_specs=(P("gz", "gy", None), P("gz", "gy", None)),
        check_vma=False,
    )
```

```python
import functools

import jax
import jax.numpy as jnp
import numpy as np
from jax import lax
from jax.experimental import pallas as pl
from jax.experimental.pallas import tpu as pltpu
from jax.sharding import PartitionSpec as P

RADIUS = 128
LANES = 128
ROWS = 8
WIDE = 256


def log_kernel(row_count, col_count, offset, radius):
    apart = np.arange(row_count)[:, None] - offset - np.arange(col_count)[None, :]
    distance = apart.astype(np.float32)
    inside = np.abs(apart) <= radius
    return np.where(inside, np.exp(-2.0 * distance * distance / float(radius * radius)), 0.0).astype(np.float32)


def halves(values):
    high = values.astype(jnp.bfloat16)
    low = (values - high.astype(jnp.float32)).astype(jnp.bfloat16)
    return high, low


def table_halves(table):
    high = table.astype(jnp.bfloat16)
    return high, (table - high.astype(np.float32)).astype(jnp.bfloat16)


def table_rows(table):
    return np.concatenate(table_halves(table), axis=0)


def table_cols(table):
    high, low = table_halves(table)
    return np.concatenate([high, high, low], axis=1)


def dot(left, right):
    return jnp.dot(left, right, preferred_element_type=jnp.float32)


def proximal(logs, outer_field):
    shifted = logs - 0.5 * outer_field
    softer = jnp.maximum(shifted, 0.0) + jnp.log(1.0 + jnp.exp(-jnp.abs(shifted)))
    exp_level = 1.0 + softer
    log_level = jnp.log(exp_level)
    log_level = log_level - (log_level + exp_level - shifted) / (1.0 + exp_level)
    exp_level = jnp.exp(log_level)
    log_level = log_level - (log_level + exp_level - shifted) / (1.0 + exp_level)
    return log_level - logs, log_level


def finish(turned, outer, at, r, out_at, dual, density):
    for k in range(at[1] // WIDE):
        there = pl.ds(pl.multiple_of(at[0] + k * WIDE, WIDE), WIDE)
        put = pl.ds(pl.multiple_of(out_at + k * WIDE, WIDE), WIDE)
        dual_part, density_part = proximal(turned(k).T, outer[r, :, there])
        dual[r, :, put] = dual_part
        density[r, :, put] = density_part


def end_kernel(done_dual, done_density, rest, outer, dual, density, rest_in, outer_in, dual_in, density_in, sems):
    depth, own_rows, length = outer.shape
    width = outer_in.shape[-1]
    before = length - width
    last = pl.ds(depth - 1, 1)
    late = [
        pltpu.make_async_copy(rest, rest_in, sems.at[0]),
        pltpu.make_async_copy(outer.at[last, :, pl.ds(before, width)], outer_in, sems.at[1]),
    ]
    for copy in late:
        copy.start()
    out = []
    for i, (source, target) in enumerate(((done_dual, dual), (done_density, density))):
        whole = pl.ds(0, depth - 1)
        out.append(pltpu.make_async_copy(source.at[whole], target.at[whole], sems.at[2 + i]))
        some = (last, slice(None), pl.ds(0, before))
        out.append(pltpu.make_async_copy(source.at[some], target.at[some], sems.at[4 + i]))
    for copy in out:
        copy.start()
    for copy in late:
        copy.wait()

    def turned(k):
        return rest_in[8 * k:8 * k + 8].reshape(WIDE, LANES)

    finish(turned, outer_in, (0, width), 0, 0, dual_in, density_in)
    for i, (source, target) in enumerate(((dual_in, dual), (density_in, density))):
        copy = pltpu.make_async_copy(source, target.at[last, :, pl.ds(before, width)], sems.at[6 + i])
        copy.start()
        out.append(copy)
    for copy in out:
        copy.wait()


MESH = pl.DeviceIdType.MESH
CHUNKS = 4
RING = 16
GROUPS = 4
EMPTY = -1e30


def chain_kernel(
    potential,
    outer,
    x_source,
    y_source,
    z_source,
    done_dual,
    done_density,
    rest,
    cells,
    a,
    b,
    c,
    d,
    e,
    f,
    home,
    outer_in,
    dual_in,
    density_in,
    x_table,
    y_table,
    z_table,
    load_sem,
    send_sem,
    recv_sem,
    own_sem,
    out_sem,
):
    depth, own_rows, length = potential.shape
    slab, part = lax.axis_index("gz"), lax.axis_index("gy")
    spot, lane = slab // GROUPS, slab % GROUPS
    core = part % 2
    level = (part // 2) * 4 + lane
    sign = 1 - 2 * core
    step_x = length // CHUNKS
    tile = a.shape[2]

    early = step_x + LANES
    loads = [
        pltpu.make_async_copy(potential.at[:, :, pl.ds(0, early)], cells.at[:, :, pl.ds(LANES, early)], load_sem.at[0]),
        pltpu.make_async_copy(
            potential.at[:, :, pl.ds(early, length - early)],
            cells.at[:, :, pl.ds(LANES + early, length - early)],
            load_sem.at[1],
        ),
        pltpu.make_async_copy(outer, outer_in, load_sem.at[2]),
    ]
    tables = [
        pltpu.make_async_copy(source, target, load_sem.at[3 + i])
        for i, (source, target) in enumerate(((x_source, x_table), (y_source, y_table), (z_source, z_table)))
    ]
    for load in loads[:1] + tables + loads[1:]:
        load.start()

    def z_peer(s):
        k = (s - 1) // 2
        away = 4 + (1 - 2 * (k % 2)) * ((k + 1) // 2)
        to_level = (level + sign * away + 8) % 8
        to_core = (core + s % 2) % 2
        return spot * GROUPS + to_level % 4, (to_level // 4) * 2 + to_core

    def xy_peer(s):
        t = (s * 5) % RING
        to_x = (spot // 4 + sign * (t % 4) + 4) % 4
        to_y = (spot % 4 + sign * (t // 4) + 4) % 4
        return to_x * 4 + to_y

    barrier = pltpu.get_barrier_semaphore()

    @pl.loop(1, RING)
    def _(s):
        pl.semaphore_signal(barrier, inc=1, device_id=z_peer(s), device_id_type=MESH)
        pl.semaphore_signal(barrier, inc=1, device_id=(xy_peer(s) * GROUPS + lane, part), device_id_type=MESH)

    def order(slab_of, part_of):
        return ((part_of // 2) * 4 + slab_of % GROUPS) * 2 + part_of % 2

    mine = order(slab, part)
    slot = lane * GROUPS + part

    def send(source, target, stage, chunk, device):
        pltpu.make_async_remote_copy(
            src_ref=source,
            dst_ref=target,
            send_sem=send_sem.at[stage, chunk],
            recv_sem=recv_sem.at[stage, chunk],
            device_id=device,
            device_id_type=MESH,
        ).start()

    def keep(source, target, stage, chunk):
        return pltpu.make_async_copy(source, target, own_sem.at[stage, chunk])

    def x_row(chunk, r):
        peaks, weights = [], []
        for k in range(6):
            at = pl.multiple_of(chunk * step_x + k * LANES, LANES)
            block = cells[r, :, pl.ds(at, LANES)]
            peak = jnp.max(block, axis=1, keepdims=True)
            peaks.append(peak)
            weights.append(jnp.exp(block - peak))
        size = 4 * LANES
        for k in range(2):
            near = range(2 * k, 2 * k + 4)
            top = peaks[near[0]]
            for j in near[1:]:
                top = jnp.maximum(top, peaks[j])
            window = jnp.concatenate([weights[j] * jnp.exp(peaks[j] - top) for j in near], axis=1)
            high, low = halves(window)
            summed = (
                dot(high, x_table[:size, :]) + dot(low, x_table[:size, :]) + dot(high, x_table[size:, :])
            )
            turned = (jnp.log(summed) + top).T
            a[chunk, 8 * k:8 * k + 8, pl.ds(pl.multiple_of(r * 32, 32), 32), :] = turned.reshape(8, 32, LANES)

    def x_send(chunk, r=None):
        rows = pl.ds(0, tile) if r is None else pl.ds(r * 32, 32)

        @pl.loop(1, RING)
        def _(s):
            to = z_peer(s)
            send(a.at[chunk, order(*to), rows], b.at[chunk, slot, rows], 0, chunk, to)

    def arrive(stage, chunk, source, target):
        view = pltpu.make_async_remote_copy(
            src_ref=source,
            dst_ref=target,
            send_sem=send_sem.at[stage, chunk],
            recv_sem=recv_sem.at[stage, chunk],
            device_id=(slab, part),
            device_id_type=MESH,
        )
        return view

    def y_stage(chunk):
        keep(a.at[chunk, mine], b.at[chunk, slot], 0, chunk).wait()
        arrive(0, chunk, a.at[chunk, pl.ds(0, RING - 1)], b.at[chunk, pl.ds(0, RING - 1)]).wait_recv()
        size = 3 * LANES

        @pl.loop(0, GROUPS)
        def _(lo):
            peaks, weights = [], []
            for k in range(GROUPS):
                block = b[chunk, lo * GROUPS + k]
                peak = jnp.max(block, axis=1, keepdims=True)
                peaks.append(peak)
                weights.append(jnp.exp(block - peak))
            for k in range(GROUPS):
                near = [j for j in range(k - 1, k + 2) if 0 <= j < GROUPS]
                top = peaks[near[0]]
                for j in near[1:]:
                    top = jnp.maximum(top, peaks[j])
                window = jnp.concatenate([weights[j] * jnp.exp(peaks[j] - top) for j in near], axis=1)
                high, low = halves(window)
                start = (near[0] - (k - 1)) * LANES
                width = len(near) * LANES
                tall = [y_table[i * size + start:i * size + start + width, :] for i in range(2)]
                logs = jnp.log(dot(high, tall[0]) + dot(low, tall[0]) + dot(high, tall[1])) + top
                for r in range(depth):
                    for g in range(4):
                        at = pl.multiple_of((lo * depth + r) * ROWS, ROWS)
                        first = (r * 4 + g) * ROWS
                        c[chunk, k * 4 + g, pl.ds(at, ROWS), :] = logs[first:first + ROWS, :]

        rows = pl.ds(pl.multiple_of(spot * tile, tile), tile)
        keep(c.at[chunk, spot], d.at[chunk, rows], 1, chunk).start()

        @pl.loop(1, RING)
        def _(s):
            to = xy_peer(s)
            send(c.at[chunk, to], d.at[chunk, rows], 1, chunk, (to * GROUPS + lane, part))

    def z_stage(chunk):
        rows = pl.ds(pl.multiple_of(spot * tile, tile), tile)
        keep(c.at[chunk, spot], d.at[chunk, rows], 1, chunk).wait()
        arrive(1, chunk, c.at[chunk, pl.ds(0, RING - 1)], d.at[chunk, pl.ds(0, (RING - 1) * tile)]).wait_recv()
        deep = RING * tile // ROWS
        tops = jnp.max(d[chunk].reshape(deep, ROWS, LANES), axis=0)
        for x in range(0, ROWS, 2):
            top = jnp.concatenate([tops[x:x + 1, :], tops[x + 1:x + 2, :]], axis=1)
            pair = jnp.concatenate([d[chunk, pl.ds(x + i, deep, stride=ROWS), :] for i in range(2)], axis=1)
            high, low = halves(jnp.exp(pair - top))
            logs = jnp.log(dot(z_table[...], jnp.concatenate([high, low, high], axis=0))) + top
            for i in range(2):
                e[chunk, pl.ds(x + i, deep, stride=ROWS), :] = logs[:, i * LANES:(i + 1) * LANES]
        keep(e.at[chunk, rows], f.at[chunk, spot], 2, chunk).start()

        @pl.loop(1, RING)
        def _(s):
            to = xy_peer(s)
            there = pl.ds(pl.multiple_of(to * tile, tile), tile)
            send(e.at[chunk, there], f.at[chunk, spot], 2, chunk, (to * GROUPS + lane, part))

    def piece(chunk, slab_of, part_of):
        rows = tile // GROUPS
        at = pl.multiple_of((slab_of % GROUPS) * rows, rows)
        return f.at[chunk, pl.ds(part_of * 4, 4), pl.ds(at, rows)]

    def back_wait(chunk):
        rows = pl.ds(pl.multiple_of(spot * tile, tile), tile)
        keep(e.at[chunk, rows], f.at[chunk, spot], 2, chunk).wait()
        arrive(2, chunk, e.at[chunk, pl.ds(0, (RING - 1) * tile)], f.at[chunk, pl.ds(0, RING - 1)]).wait_recv()

    def back_send(source, target, stage, column):
        keep(source(slab, part), target, stage, column).start()

        @pl.loop(1, RING)
        def _(s):
            to = z_peer(s)
            send(source(*to), target, stage, column, to)

    def back_stage(chunk):
        back_wait(chunk)
        back_send(functools.partial(piece, chunk), home.at[chunk, mine], 3, chunk)

    final = CHUNKS - 1

    def row_piece(r, slab_of, part_of):
        at = pl.multiple_of((slab_of % GROUPS) * (tile // GROUPS) + r * ROWS, ROWS)
        return f.at[final, pl.ds(part_of * 4, 4), pl.ds(at, ROWS)]

    def row_place(r, which):
        return rest.at[which] if r == depth - 1 else home.at[final, which, :, pl.ds(r * ROWS, ROWS)]

    row_sems = [(3, final)] + [(4, r - 1) for r in range(1, depth)]

    edge = jnp.full((depth, own_rows, LANES), EMPTY, jnp.float32)
    cells[:, :, :LANES] = edge
    cells[:, :, LANES + length:] = edge
    loads[0].wait()
    tables[0].wait()
    for r in range(depth):
        x_row(0, r)
        if r == 0:
            pl.semaphore_wait(barrier, 2 * (RING - 1))
        x_send(0, r)
    keep(a.at[0, mine], b.at[0, slot], 0, 0).start()
    for load in loads[1:2] + tables[1:]:
        load.wait()

    @pl.loop(1, CHUNKS)
    def _(chunk):
        @pl.loop(0, depth)
        def _(r):
            x_row(chunk, r)

        keep(a.at[chunk, mine], b.at[chunk, slot], 0, chunk).start()
        x_send(chunk)

    @pl.loop(0, CHUNKS)
    def _(chunk):
        y_stage(chunk)

        @pl.when(chunk > 0)
        def _():
            back_stage(chunk - 1)

        z_stage(chunk)

    back_wait(final)
    for r in range(depth):
        back_send(functools.partial(row_piece, r), row_place(r, mine), *row_sems[r])
    loads[2].wait()
    some = pl.ds(0, RING - 1)

    def out_copies(rows, chunk, column):
        at = pl.ds(pl.multiple_of(chunk * step_x, step_x), step_x)
        return [
            pltpu.make_async_copy(source.at[rows, :, at], target.at[rows, :, at], out_sem.at[i, column])
            for i, (source, target) in enumerate(((dual_in, done_dual), (density_in, done_density)))
        ]

    every = pl.ds(0, depth)

    def row(chunk, r):
        def turned(k):
            rows = pl.ds(pl.multiple_of(r * ROWS, ROWS), ROWS)
            return home[chunk, 8 * k:8 * k + 8, :, rows, :].reshape(WIDE, LANES)

        finish(turned, outer_in, (chunk * step_x, step_x), r, chunk * step_x, dual_in, density_in)

    @pl.loop(0, final)
    def _(chunk):
        keep(piece(chunk, slab, part), home.at[chunk, mine], 3, chunk).wait()
        arrive(3, chunk, home.at[chunk, some], home.at[chunk, some]).wait_recv()

        @pl.loop(0, depth)
        def _(r):
            row(chunk, r)

        for copy in out_copies(every, chunk, chunk):
            copy.start()

    for r in range(depth):
        keep(row_piece(r, slab, part), row_place(r, mine), *row_sems[r]).wait()
        if r == depth - 1:
            break
        arrive(*row_sems[r], row_place(r, some), row_place(r, some)).wait_recv()
        row(final, r)
        for copy in out_copies(pl.ds(r, 1), final, final + r):
            copy.start()

    @pl.loop(0, final)
    def _(chunk):
        for copy in out_copies(every, chunk, chunk):
            copy.wait()

    for r in range(depth - 1):
        for copy in out_copies(pl.ds(r, 1), final, final + r):
            copy.wait()

    @pl.loop(0, CHUNKS)
    def _(chunk):
        flat = pl.ds(0, (RING - 1) * tile)
        arrive(0, chunk, a.at[chunk, some], b.at[chunk, some]).wait_send()
        arrive(1, chunk, c.at[chunk, some], d.at[chunk, flat]).wait_send()
        arrive(2, chunk, e.at[chunk, flat], f.at[chunk, some]).wait_send()

    @pl.loop(0, final)
    def _(chunk):
        arrive(3, chunk, home.at[chunk, some], home.at[chunk, some]).wait_send()

    for r in range(depth):
        arrive(*row_sems[r], row_place(r, some), row_place(r, some)).wait_send()
    arrive(*row_sems[-1], row_place(depth - 1, some), row_place(depth - 1, some)).wait_recv()


def local(potential, external):
    depth, own_rows, length = potential.shape
    groups = lax.axis_size("gz")
    rows = depth * ROWS
    tile = GROUPS * rows
    wide = length // CHUNKS
    anywhere = pl.BlockSpec(memory_space=pl.ANY)
    x_table = jnp.asarray(table_rows(log_kernel(4 * LANES, WIDE, RADIUS, RADIUS)))
    y_table = jnp.asarray(table_rows(log_kernel(3 * LANES, LANES, RADIUS, RADIUS)))
    z_table = jnp.asarray(table_cols(log_kernel(groups * depth, groups * depth, 0, RADIUS)))
    stack = pltpu.VMEM((CHUNKS, RING, tile, LANES), jnp.float32)
    long = pltpu.VMEM((CHUNKS, RING * tile, LANES), jnp.float32)
    field = jax.ShapeDtypeStruct(potential.shape, jnp.float32)
    held = pltpu.VMEM(potential.shape, jnp.float32)
    piece = (RING, GROUPS, ROWS, LANES)
    done_dual, done_density, rest = pl.pallas_call(
        chain_kernel,
        out_shape=(field, field, jax.ShapeDtypeStruct(piece, jnp.float32)),
        in_specs=[pl.BlockSpec(memory_space=pltpu.HBM)] * 5,
        out_specs=(anywhere, anywhere, anywhere),
        scratch_shapes=[
            pltpu.VMEM((depth, own_rows, length + 2 * LANES), jnp.float32),
            stack,
            stack,
            stack,
            long,
            long,
            stack,
            pltpu.VMEM((CHUNKS, RING, GROUPS, rows, LANES), jnp.float32),
            held,
            held,
            held,
            *[pltpu.VMEM(table.shape, table.dtype) for table in (x_table, y_table, z_table)],
            pltpu.SemaphoreType.DMA((6,)),
            pltpu.SemaphoreType.DMA((5, CHUNKS)),
            pltpu.SemaphoreType.DMA((5, CHUNKS)),
            pltpu.SemaphoreType.DMA((5, CHUNKS)),
            pltpu.SemaphoreType.DMA((2, CHUNKS - 1 + depth)),
        ],
        compiler_params=pltpu.CompilerParams(collective_id=0, has_side_effects=True, vmem_limit_bytes=44 << 20),
        name="along_xyz",
    )(*[pltpu.with_memory_space_constraint(v, pltpu.HBM) for v in (potential, external, x_table, y_table, z_table)])
    late = pltpu.VMEM((1, own_rows, wide), jnp.float32)
    return pl.pallas_call(
        end_kernel,
        out_shape=(field, field),
        in_specs=[anywhere] * 3 + [pl.BlockSpec(memory_space=pltpu.HBM)],
        out_specs=(anywhere, anywhere),
        scratch_shapes=[pltpu.VMEM(piece, jnp.float32), late, late, late, pltpu.SemaphoreType.DMA((8,))],
        compiler_params=pltpu.CompilerParams(vmem_limit_bytes=16 << 20),
        name="proximal",
    )(done_dual, done_density, rest, pltpu.with_memory_space_constraint(external, pltpu.HBM))


def solution(mesh):
    return jax.shard_map(
        local,
        mesh=mesh,
        in_specs=(P("gz", "gy", None), P("gz", "gy", None)),
        out_specs=(P("gz", "gy", None), P("gz", "gy", None)),
        check_vma=False,
    )
```

```python
import functools

import jax
import jax.numpy as jnp
import numpy as np
from jax import lax
from jax.experimental import pallas as pl
from jax.experimental.pallas import tpu as pltpu
from jax.sharding import PartitionSpec as P

RADIUS = 128
LANES = 128
ROWS = 8
WIDE = 256


def log_kernel(row_count, col_count, offset, radius):
    apart = np.arange(row_count)[:, None] - offset - np.arange(col_count)[None, :]
    distance = apart.astype(np.float32)
    inside = np.abs(apart) <= radius
    return np.where(inside, np.exp(-2.0 * distance * distance / float(radius * radius)), 0.0).astype(np.float32)


def halves(values):
    high = values.astype(jnp.bfloat16)
    low = (values - high.astype(jnp.float32)).astype(jnp.bfloat16)
    return high, low


def table_halves(table):
    high = table.astype(jnp.bfloat16)
    return high, (table - high.astype(np.float32)).astype(jnp.bfloat16)


def table_rows(table):
    return np.concatenate(table_halves(table), axis=0)


def table_cols(table):
    high, low = table_halves(table)
    return np.concatenate([high, high, low], axis=1)


def dot(left, right):
    return jnp.dot(left, right, preferred_element_type=jnp.float32)


def proximal(logs, outer_field):
    shifted = logs - 0.5 * outer_field
    softer = jnp.maximum(shifted, 0.0) + jnp.log(1.0 + jnp.exp(-jnp.abs(shifted)))
    exp_level = 1.0 + softer
    log_level = jnp.log(exp_level)
    log_level = log_level - (log_level + exp_level - shifted) / (1.0 + exp_level)
    exp_level = jnp.exp(log_level)
    log_level = log_level - (log_level + exp_level - shifted) / (1.0 + exp_level)
    return log_level - logs, log_level


def finish(turned, outer, at, r, out_at, dual, density):
    for k in range(at[1] // WIDE):
        there = pl.ds(pl.multiple_of(at[0] + k * WIDE, WIDE), WIDE)
        put = pl.ds(pl.multiple_of(out_at + k * WIDE, WIDE), WIDE)
        dual_part, density_part = proximal(turned(k).T, outer[r, :, there])
        dual[r, :, put] = dual_part
        density[r, :, put] = density_part


def end_kernel(done_dual, done_density, rest, outer, dual, density, rest_in, outer_in, dual_in, density_in, sems):
    depth, own_rows, length = outer.shape
    width = outer_in.shape[-1]
    before = length - width
    last = pl.ds(depth - 1, 1)
    late = [
        pltpu.make_async_copy(rest, rest_in, sems.at[0]),
        pltpu.make_async_copy(outer.at[last, :, pl.ds(before, width)], outer_in, sems.at[1]),
    ]
    for copy in late:
        copy.start()
    out = []
    for i, (source, target) in enumerate(((done_dual, dual), (done_density, density))):
        whole = pl.ds(0, depth - 1)
        out.append(pltpu.make_async_copy(source.at[whole], target.at[whole], sems.at[2 + i]))
        some = (last, slice(None), pl.ds(0, before))
        out.append(pltpu.make_async_copy(source.at[some], target.at[some], sems.at[4 + i]))
    for copy in out:
        copy.start()
    for copy in late:
        copy.wait()

    def turned(k):
        return rest_in[8 * k:8 * k + 8].reshape(WIDE, LANES)

    finish(turned, outer_in, (0, width), 0, 0, dual_in, density_in)
    for i, (source, target) in enumerate(((dual_in, dual), (density_in, density))):
        copy = pltpu.make_async_copy(source, target.at[last, :, pl.ds(before, width)], sems.at[6 + i])
        copy.start()
        out.append(copy)
    for copy in out:
        copy.wait()


MESH = pl.DeviceIdType.MESH
CHUNKS = 4
RING = 16
GROUPS = 4
EMPTY = -1e30


def chain_kernel(
    potential,
    outer,
    x_source,
    y_source,
    z_source,
    done_dual,
    done_density,
    rest,
    cells,
    a,
    b,
    c,
    d,
    e,
    f,
    home,
    outer_in,
    dual_in,
    density_in,
    x_table,
    y_table,
    z_table,
    load_sem,
    send_sem,
    recv_sem,
    own_sem,
    out_sem,
    z_ready,
    xy_ready,
):
    depth, own_rows, length = potential.shape
    slab, part = lax.axis_index("gz"), lax.axis_index("gy")
    spot, lane = slab // GROUPS, slab % GROUPS
    core = part % 2
    level = (part // 2) * 4 + lane
    sign = 1 - 2 * core
    step_x = length // CHUNKS
    tile = a.shape[2]

    early = step_x + LANES
    loads = [
        pltpu.make_async_copy(potential.at[:, :, pl.ds(0, early)], cells.at[:, :, pl.ds(LANES, early)], load_sem.at[0]),
        pltpu.make_async_copy(
            potential.at[:, :, pl.ds(early, length - early)],
            cells.at[:, :, pl.ds(LANES + early, length - early)],
            load_sem.at[1],
        ),
        pltpu.make_async_copy(outer, outer_in, load_sem.at[2]),
    ]
    tables = [
        pltpu.make_async_copy(source, target, load_sem.at[3 + i])
        for i, (source, target) in enumerate(((x_source, x_table), (y_source, y_table), (z_source, z_table)))
    ]
    for load in loads[:1] + tables + loads[1:]:
        load.start()

    def z_peer(s):
        k = (s - 1) // 2
        away = 4 + (1 - 2 * (k % 2)) * ((k + 1) // 2)
        to_level = (level + sign * away + 8) % 8
        to_core = (core + s % 2) % 2
        return spot * GROUPS + to_level % 4, (to_level // 4) * 2 + to_core

    def xy_peer(s):
        t = (s * 5) % RING
        to_x = (spot // 4 + sign * (t % 4) + 4) % 4
        to_y = (spot % 4 + sign * (t // 4) + 4) % 4
        return to_x * 4 + to_y

    barrier = pltpu.get_barrier_semaphore()

    first, second = (slab, part - core), (slab, part - core + 1)

    @pl.loop(1, 8)
    def _(s):
        to_level = (level + s) % 8
        to = spot * GROUPS + to_level % 4, (to_level // 4) * 2
        pl.semaphore_signal(barrier, inc=1, device_id=to, device_id_type=MESH)

    @pl.when(core == 1)
    def _():
        pl.semaphore_signal(barrier, inc=1, device_id=first, device_id_type=MESH)

    @pl.loop(1, RING)
    def _(s):
        to = xy_peer(s) * GROUPS + lane, part - core + 1
        pl.semaphore_signal(barrier, inc=1, device_id=to, device_id_type=MESH)

    def meet_z():
        @pl.when(core == 0)
        def _():
            pl.semaphore_wait(barrier, RING - 1)
            pl.semaphore_signal(z_ready, inc=1, device_id=second, device_id_type=MESH)

        @pl.when(core == 1)
        def _():
            pl.semaphore_wait(z_ready, 1)

    def meet_xy():
        @pl.when(core == 1)
        def _():
            pl.semaphore_wait(barrier, 2 * (RING - 1))
            pl.semaphore_signal(xy_ready, inc=1, device_id=first, device_id_type=MESH)

        @pl.when(core == 0)
        def _():
            pl.semaphore_wait(xy_ready, 1)

    def order(slab_of, part_of):
        return ((part_of // 2) * 4 + slab_of % GROUPS) * 2 + part_of % 2

    mine = order(slab, part)
    slot = lane * GROUPS + part

    def send(source, target, stage, chunk, device):
        pltpu.make_async_remote_copy(
            src_ref=source,
            dst_ref=target,
            send_sem=send_sem.at[stage, chunk],
            recv_sem=recv_sem.at[stage, chunk],
            device_id=device,
            device_id_type=MESH,
        ).start()

    def keep(source, target, stage, chunk):
        return pltpu.make_async_copy(source, target, own_sem.at[stage, chunk])

    def x_row(chunk, r):
        peaks, weights = [], []
        for k in range(6):
            at = pl.multiple_of(chunk * step_x + k * LANES, LANES)
            block = cells[r, :, pl.ds(at, LANES)]
            peak = jnp.max(block, axis=1, keepdims=True)
            peaks.append(peak)
            weights.append(jnp.exp(block - peak))
        size = 4 * LANES
        for k in range(2):
            near = range(2 * k, 2 * k + 4)
            top = peaks[near[0]]
            for j in near[1:]:
                top = jnp.maximum(top, peaks[j])
            window = jnp.concatenate([weights[j] * jnp.exp(peaks[j] - top) for j in near], axis=1)
            high, low = halves(window)
            summed = (
                dot(high, x_table[:size, :]) + dot(low, x_table[:size, :]) + dot(high, x_table[size:, :])
            )
            turned = (jnp.log(summed) + top).T
            a[chunk, 8 * k:8 * k + 8, pl.ds(pl.multiple_of(r * 32, 32), 32), :] = turned.reshape(8, 32, LANES)

    def x_send(chunk, r=None):
        rows = pl.ds(0, tile) if r is None else pl.ds(r * 32, 32)

        @pl.loop(1, RING)
        def _(s):
            to = z_peer(s)
            send(a.at[chunk, order(*to), rows], b.at[chunk, slot, rows], 0, chunk, to)

    def arrive(stage, chunk, source, target):
        view = pltpu.make_async_remote_copy(
            src_ref=source,
            dst_ref=target,
            send_sem=send_sem.at[stage, chunk],
            recv_sem=recv_sem.at[stage, chunk],
            device_id=(slab, part),
            device_id_type=MESH,
        )
        return view

    def y_stage(chunk):
        keep(a.at[chunk, mine], b.at[chunk, slot], 0, chunk).wait()
        arrive(0, chunk, a.at[chunk, pl.ds(0, RING - 1)], b.at[chunk, pl.ds(0, RING - 1)]).wait_recv()
        size = 3 * LANES

        @pl.loop(0, GROUPS)
        def _(lo):
            peaks, weights = [], []
            for k in range(GROUPS):
                block = b[chunk, lo * GROUPS + k]
                peak = jnp.max(block, axis=1, keepdims=True)
                peaks.append(peak)
                weights.append(jnp.exp(block - peak))
            for k in range(GROUPS):
                near = [j for j in range(k - 1, k + 2) if 0 <= j < GROUPS]
                top = peaks[near[0]]
                for j in near[1:]:
                    top = jnp.maximum(top, peaks[j])
                window = jnp.concatenate([weights[j] * jnp.exp(peaks[j] - top) for j in near], axis=1)
                high, low = halves(window)
                start = (near[0] - (k - 1)) * LANES
                width = len(near) * LANES
                tall = [y_table[i * size + start:i * size + start + width, :] for i in range(2)]
                logs = jnp.log(dot(high, tall[0]) + dot(low, tall[0]) + dot(high, tall[1])) + top
                for r in range(depth):
                    for g in range(4):
                        at = pl.multiple_of((lo * depth + r) * ROWS, ROWS)
                        first = (r * 4 + g) * ROWS
                        c[chunk, k * 4 + g, pl.ds(at, ROWS), :] = logs[first:first + ROWS, :]

        rows = pl.ds(pl.multiple_of(spot * tile, tile), tile)
        keep(c.at[chunk, spot], d.at[chunk, rows], 1, chunk).start()

        @pl.loop(1, RING)
        def _(s):
            to = xy_peer(s)
            send(c.at[chunk, to], d.at[chunk, rows], 1, chunk, (to * GROUPS + lane, part))

    def z_stage(chunk):
        rows = pl.ds(pl.multiple_of(spot * tile, tile), tile)
        keep(c.at[chunk, spot], d.at[chunk, rows], 1, chunk).wait()
        arrive(1, chunk, c.at[chunk, pl.ds(0, RING - 1)], d.at[chunk, pl.ds(0, (RING - 1) * tile)]).wait_recv()
        deep = RING * tile // ROWS
        tops = jnp.max(d[chunk].reshape(deep, ROWS, LANES), axis=0)
        for x in range(0, ROWS, 2):
            top = jnp.concatenate([tops[x:x + 1, :], tops[x + 1:x + 2, :]], axis=1)
            pair = jnp.concatenate([d[chunk, pl.ds(x + i, deep, stride=ROWS), :] for i in range(2)], axis=1)
            high, low = halves(jnp.exp(pair - top))
            logs = jnp.log(dot(z_table[...], jnp.concatenate([high, low, high], axis=0))) + top
            for i in range(2):
                e[chunk, pl.ds(x + i, deep, stride=ROWS), :] = logs[:, i * LANES:(i + 1) * LANES]
        keep(e.at[chunk, rows], f.at[chunk, spot], 2, chunk).start()

        @pl.loop(1, RING)
        def _(s):
            to = xy_peer(s)
            there = pl.ds(pl.multiple_of(to * tile, tile), tile)
            send(e.at[chunk, there], f.at[chunk, spot], 2, chunk, (to * GROUPS + lane, part))

    def piece(chunk, slab_of, part_of):
        rows = tile // GROUPS
        at = pl.multiple_of((slab_of % GROUPS) * rows, rows)
        return f.at[chunk, pl.ds(part_of * 4, 4), pl.ds(at, rows)]

    def back_wait(chunk):
        rows = pl.ds(pl.multiple_of(spot * tile, tile), tile)
        keep(e.at[chunk, rows], f.at[chunk, spot], 2, chunk).wait()
        arrive(2, chunk, e.at[chunk, pl.ds(0, (RING - 1) * tile)], f.at[chunk, pl.ds(0, RING - 1)]).wait_recv()

    def back_send(source, target, stage, column):
        keep(source(slab, part), target, stage, column).start()

        @pl.loop(1, RING)
        def _(s):
            to = z_peer(s)
            send(source(*to), target, stage, column, to)

    def back_stage(chunk):
        back_wait(chunk)
        back_send(functools.partial(piece, chunk), home.at[chunk, mine], 3, chunk)

    final = CHUNKS - 1

    def row_piece(r, slab_of, part_of):
        at = pl.multiple_of((slab_of % GROUPS) * (tile // GROUPS) + r * ROWS, ROWS)
        return f.at[final, pl.ds(part_of * 4, 4), pl.ds(at, ROWS)]

    def row_place(r, which):
        return rest.at[which] if r == depth - 1 else home.at[final, which, :, pl.ds(r * ROWS, ROWS)]

    row_sems = [(3, final)] + [(4, r - 1) for r in range(1, depth)]

    edge = jnp.full((depth, own_rows, LANES), EMPTY, jnp.float32)
    cells[:, :, :LANES] = edge
    cells[:, :, LANES + length:] = edge
    loads[0].wait()
    tables[0].wait()
    for r in range(depth):
        x_row(0, r)
        if r == 0:
            meet_z()
        x_send(0, r)
    keep(a.at[0, mine], b.at[0, slot], 0, 0).start()
    for load in loads[1:2] + tables[1:]:
        load.wait()

    @pl.loop(1, CHUNKS)
    def _(chunk):
        @pl.loop(0, depth)
        def _(r):
            x_row(chunk, r)

        keep(a.at[chunk, mine], b.at[chunk, slot], 0, chunk).start()
        x_send(chunk)

    meet_xy()

    @pl.loop(0, CHUNKS)
    def _(chunk):
        y_stage(chunk)

        @pl.when(chunk > 0)
        def _():
            back_stage(chunk - 1)

        z_stage(chunk)

    back_wait(final)
    for r in range(depth):
        back_send(functools.partial(row_piece, r), row_place(r, mine), *row_sems[r])
    loads[2].wait()
    some = pl.ds(0, RING - 1)

    def out_copies(rows, chunk, column):
        at = pl.ds(pl.multiple_of(chunk * step_x, step_x), step_x)
        return [
            pltpu.make_async_copy(source.at[rows, :, at], target.at[rows, :, at], out_sem.at[i, column])
            for i, (source, target) in enumerate(((dual_in, done_dual), (density_in, done_density)))
        ]

    every = pl.ds(0, depth)

    def row(chunk, r):
        def turned(k):
            rows = pl.ds(pl.multiple_of(r * ROWS, ROWS), ROWS)
            return home[chunk, 8 * k:8 * k + 8, :, rows, :].reshape(WIDE, LANES)

        finish(turned, outer_in, (chunk * step_x, step_x), r, chunk * step_x, dual_in, density_in)

    @pl.loop(0, final)
    def _(chunk):
        keep(piece(chunk, slab, part), home.at[chunk, mine], 3, chunk).wait()
        arrive(3, chunk, home.at[chunk, some], home.at[chunk, some]).wait_recv()

        @pl.loop(0, depth)
        def _(r):
            row(chunk, r)

        for copy in out_copies(every, chunk, chunk):
            copy.start()

    for r in range(depth):
        keep(row_piece(r, slab, part), row_place(r, mine), *row_sems[r]).wait()
        if r == depth - 1:
            break
        arrive(*row_sems[r], row_place(r, some), row_place(r, some)).wait_recv()
        row(final, r)
        for copy in out_copies(pl.ds(r, 1), final, final + r):
            copy.start()

    @pl.loop(0, final)
    def _(chunk):
        for copy in out_copies(every, chunk, chunk):
            copy.wait()

    for r in range(depth - 1):
        for copy in out_copies(pl.ds(r, 1), final, final + r):
            copy.wait()

    @pl.loop(0, CHUNKS)
    def _(chunk):
        flat = pl.ds(0, (RING - 1) * tile)
        arrive(0, chunk, a.at[chunk, some], b.at[chunk, some]).wait_send()
        arrive(1, chunk, c.at[chunk, some], d.at[chunk, flat]).wait_send()
        arrive(2, chunk, e.at[chunk, flat], f.at[chunk, some]).wait_send()

    @pl.loop(0, final)
    def _(chunk):
        arrive(3, chunk, home.at[chunk, some], home.at[chunk, some]).wait_send()

    for r in range(depth):
        arrive(*row_sems[r], row_place(r, some), row_place(r, some)).wait_send()
    arrive(*row_sems[-1], row_place(depth - 1, some), row_place(depth - 1, some)).wait_recv()


def local(potential, external):
    depth, own_rows, length = potential.shape
    groups = lax.axis_size("gz")
    rows = depth * ROWS
    tile = GROUPS * rows
    wide = length // CHUNKS
    anywhere = pl.BlockSpec(memory_space=pl.ANY)
    x_table = jnp.asarray(table_rows(log_kernel(4 * LANES, WIDE, RADIUS, RADIUS)))
    y_table = jnp.asarray(table_rows(log_kernel(3 * LANES, LANES, RADIUS, RADIUS)))
    z_table = jnp.asarray(table_cols(log_kernel(groups * depth, groups * depth, 0, RADIUS)))
    stack = pltpu.VMEM((CHUNKS, RING, tile, LANES), jnp.float32)
    long = pltpu.VMEM((CHUNKS, RING * tile, LANES), jnp.float32)
    field = jax.ShapeDtypeStruct(potential.shape, jnp.float32)
    held = pltpu.VMEM(potential.shape, jnp.float32)
    piece = (RING, GROUPS, ROWS, LANES)
    done_dual, done_density, rest = pl.pallas_call(
        chain_kernel,
        out_shape=(field, field, jax.ShapeDtypeStruct(piece, jnp.float32)),
        in_specs=[pl.BlockSpec(memory_space=pltpu.HBM)] * 5,
        out_specs=(anywhere, anywhere, anywhere),
        scratch_shapes=[
            pltpu.VMEM((depth, own_rows, length + 2 * LANES), jnp.float32),
            stack,
            stack,
            stack,
            long,
            long,
            stack,
            pltpu.VMEM((CHUNKS, RING, GROUPS, rows, LANES), jnp.float32),
            held,
            held,
            held,
            *[pltpu.VMEM(table.shape, table.dtype) for table in (x_table, y_table, z_table)],
            pltpu.SemaphoreType.DMA((6,)),
            pltpu.SemaphoreType.DMA((5, CHUNKS)),
            pltpu.SemaphoreType.DMA((5, CHUNKS)),
            pltpu.SemaphoreType.DMA((5, CHUNKS)),
            pltpu.SemaphoreType.DMA((2, CHUNKS - 1 + depth)),
            pltpu.SemaphoreType.REGULAR,
            pltpu.SemaphoreType.REGULAR,
        ],
        compiler_params=pltpu.CompilerParams(collective_id=0, has_side_effects=True, vmem_limit_bytes=44 << 20),
        name="along_xyz",
    )(*[pltpu.with_memory_space_constraint(v, pltpu.HBM) for v in (potential, external, x_table, y_table, z_table)])
    late = pltpu.VMEM((1, own_rows, wide), jnp.float32)
    return pl.pallas_call(
        end_kernel,
        out_shape=(field, field),
        in_specs=[anywhere] * 3 + [pl.BlockSpec(memory_space=pltpu.HBM)],
        out_specs=(anywhere, anywhere),
        scratch_shapes=[pltpu.VMEM(piece, jnp.float32), late, late, late, pltpu.SemaphoreType.DMA((8,))],
        compiler_params=pltpu.CompilerParams(vmem_limit_bytes=16 << 20),
        name="proximal",
    )(done_dual, done_density, rest, pltpu.with_memory_space_constraint(external, pltpu.HBM))


def solution(mesh):
    return jax.shard_map(
        local,
        mesh=mesh,
        in_specs=(P("gz", "gy", None), P("gz", "gy", None)),
        out_specs=(P("gz", "gy", None), P("gz", "gy", None)),
        check_vma=False,
    )
```

```python
import functools

import jax
import jax.numpy as jnp
import numpy as np
from jax import lax
from jax.experimental import pallas as pl
from jax.experimental.pallas import tpu as pltpu
from jax.sharding import PartitionSpec as P

RADIUS = 128
LANES = 128
ROWS = 8
WIDE = 256


def log_kernel(row_count, col_count, offset, radius):
    apart = np.arange(row_count)[:, None] - offset - np.arange(col_count)[None, :]
    distance = apart.astype(np.float32)
    inside = np.abs(apart) <= radius
    return np.where(inside, np.exp(-2.0 * distance * distance / float(radius * radius)), 0.0).astype(np.float32)


def halves(values):
    high = values.astype(jnp.bfloat16)
    low = (values - high.astype(jnp.float32)).astype(jnp.bfloat16)
    return high, low


def table_halves(table):
    high = table.astype(jnp.bfloat16)
    return high, (table - high.astype(np.float32)).astype(jnp.bfloat16)


def table_rows(table):
    return np.concatenate(table_halves(table), axis=0)


def table_cols(table):
    high, low = table_halves(table)
    return np.concatenate([high, high, low], axis=1)


def dot(left, right):
    return jnp.dot(left, right, preferred_element_type=jnp.float32)


def proximal(logs, outer_field):
    shifted = logs - 0.5 * outer_field
    softer = jnp.maximum(shifted, 0.0) + jnp.log(1.0 + jnp.exp(-jnp.abs(shifted)))
    exp_level = 1.0 + softer
    log_level = jnp.log(exp_level)
    log_level = log_level - (log_level + exp_level - shifted) / (1.0 + exp_level)
    exp_level = jnp.exp(log_level)
    log_level = log_level - (log_level + exp_level - shifted) / (1.0 + exp_level)
    return log_level - logs, log_level


def finish(turned, outer, at, r, out_at, dual, density):
    for k in range(at[1] // WIDE):
        there = pl.ds(pl.multiple_of(at[0] + k * WIDE, WIDE), WIDE)
        put = pl.ds(pl.multiple_of(out_at + k * WIDE, WIDE), WIDE)
        dual_part, density_part = proximal(turned(k).T, outer[r, :, there])
        dual[r, :, put] = dual_part
        density[r, :, put] = density_part


def end_kernel(done_dual, done_density, rest, outer, dual, density, rest_in, outer_in, dual_in, density_in, sems):
    depth, own_rows, length = dual.shape
    width = outer_in.shape[-1]
    before = length - width
    last = pl.ds(depth - 1, 1)
    late = [
        pltpu.make_async_copy(rest, rest_in, sems.at[0]),
        pltpu.make_async_copy(outer, outer_in, sems.at[1]),
    ]
    for copy in late:
        copy.start()
    out = []
    for i, (source, target) in enumerate(((done_dual, dual), (done_density, density))):
        whole = pl.ds(0, depth - 1)
        out.append(pltpu.make_async_copy(source.at[whole], target.at[whole], sems.at[2 + i]))
        some = (last, slice(None), pl.ds(0, before))
        out.append(pltpu.make_async_copy(source.at[some], target.at[some], sems.at[4 + i]))
    for copy in out:
        copy.start()
    for copy in late:
        copy.wait()

    def turned(k):
        return rest_in[8 * k:8 * k + 8].reshape(WIDE, LANES)

    finish(turned, outer_in, (0, width), 0, 0, dual_in, density_in)
    for i, (source, target) in enumerate(((dual_in, dual), (density_in, density))):
        copy = pltpu.make_async_copy(source, target.at[last, :, pl.ds(before, width)], sems.at[6 + i])
        copy.start()
        out.append(copy)
    for copy in out:
        copy.wait()


MESH = pl.DeviceIdType.MESH
CHUNKS = 4
RING = 16
GROUPS = 4
EMPTY = -1e30


def chain_kernel(
    potential,
    outer,
    x_source,
    y_source,
    z_source,
    done_dual,
    done_density,
    rest,
    rest_outer,
    cells,
    a,
    b,
    c,
    d,
    e,
    f,
    home,
    outer_in,
    dual_in,
    density_in,
    x_table,
    y_table,
    z_table,
    load_sem,
    send_sem,
    recv_sem,
    own_sem,
    out_sem,
    z_ready,
    xy_ready,
):
    depth, own_rows, length = potential.shape
    slab, part = lax.axis_index("gz"), lax.axis_index("gy")
    spot, lane = slab // GROUPS, slab % GROUPS
    core = part % 2
    level = (part // 2) * 4 + lane
    sign = 1 - 2 * core
    step_x = length // CHUNKS
    tile = a.shape[2]

    early = step_x + LANES
    loads = [
        pltpu.make_async_copy(potential.at[:, :, pl.ds(0, early)], cells.at[:, :, pl.ds(LANES, early)], load_sem.at[0]),
        pltpu.make_async_copy(
            potential.at[:, :, pl.ds(early, length - early)],
            cells.at[:, :, pl.ds(LANES + early, length - early)],
            load_sem.at[1],
        ),
        pltpu.make_async_copy(outer, outer_in, load_sem.at[2]),
    ]
    tables = [
        pltpu.make_async_copy(source, target, load_sem.at[3 + i])
        for i, (source, target) in enumerate(((x_source, x_table), (y_source, y_table), (z_source, z_table)))
    ]
    for load in loads[:1] + tables + loads[1:]:
        load.start()

    def z_peer(s):
        k = (s - 1) // 2
        away = 4 + (1 - 2 * (k % 2)) * ((k + 1) // 2)
        to_level = (level + sign * away + 8) % 8
        to_core = (core + s % 2) % 2
        return spot * GROUPS + to_level % 4, (to_level // 4) * 2 + to_core

    def xy_peer(s):
        t = (s * 5) % RING
        to_x = (spot // 4 + sign * (t % 4) + 4) % 4
        to_y = (spot % 4 + sign * (t // 4) + 4) % 4
        return to_x * 4 + to_y

    barrier = pltpu.get_barrier_semaphore()

    first, second = (slab, part - core), (slab, part - core + 1)

    @pl.loop(1, 8)
    def _(s):
        to_level = (level + s) % 8
        to = spot * GROUPS + to_level % 4, (to_level // 4) * 2
        pl.semaphore_signal(barrier, inc=1, device_id=to, device_id_type=MESH)

    @pl.when(core == 1)
    def _():
        pl.semaphore_signal(barrier, inc=1, device_id=first, device_id_type=MESH)

    @pl.loop(1, RING)
    def _(s):
        to = xy_peer(s) * GROUPS + lane, part - core + 1
        pl.semaphore_signal(barrier, inc=1, device_id=to, device_id_type=MESH)

    def meet_z():
        @pl.when(core == 0)
        def _():
            pl.semaphore_wait(barrier, RING - 1)
            pl.semaphore_signal(z_ready, inc=1, device_id=second, device_id_type=MESH)

        @pl.when(core == 1)
        def _():
            pl.semaphore_wait(z_ready, 1)

    def meet_xy():
        @pl.when(core == 1)
        def _():
            pl.semaphore_wait(barrier, 2 * (RING - 1))
            pl.semaphore_signal(xy_ready, inc=1, device_id=first, device_id_type=MESH)

        @pl.when(core == 0)
        def _():
            pl.semaphore_wait(xy_ready, 1)

    def order(slab_of, part_of):
        return ((part_of // 2) * 4 + slab_of % GROUPS) * 2 + part_of % 2

    mine = order(slab, part)
    slot = lane * GROUPS + part

    def send(source, target, stage, chunk, device):
        pltpu.make_async_remote_copy(
            src_ref=source,
            dst_ref=target,
            send_sem=send_sem.at[stage, chunk],
            recv_sem=recv_sem.at[stage, chunk],
            device_id=device,
            device_id_type=MESH,
        ).start()

    def keep(source, target, stage, chunk):
        return pltpu.make_async_copy(source, target, own_sem.at[stage, chunk])

    def x_row(chunk, r):
        peaks, weights = [], []
        for k in range(6):
            at = pl.multiple_of(chunk * step_x + k * LANES, LANES)
            block = cells[r, :, pl.ds(at, LANES)]
            peak = jnp.max(block, axis=1, keepdims=True)
            peaks.append(peak)
            weights.append(jnp.exp(block - peak))
        size = 4 * LANES
        for k in range(2):
            near = range(2 * k, 2 * k + 4)
            top = peaks[near[0]]
            for j in near[1:]:
                top = jnp.maximum(top, peaks[j])
            window = jnp.concatenate([weights[j] * jnp.exp(peaks[j] - top) for j in near], axis=1)
            high, low = halves(window)
            summed = (
                dot(high, x_table[:size, :]) + dot(low, x_table[:size, :]) + dot(high, x_table[size:, :])
            )
            turned = (jnp.log(summed) + top).T
            a[chunk, 8 * k:8 * k + 8, pl.ds(pl.multiple_of(r * 32, 32), 32), :] = turned.reshape(8, 32, LANES)

    def x_send(chunk, r=None):
        rows = pl.ds(0, tile) if r is None else pl.ds(r * 32, 32)

        @pl.loop(1, RING)
        def _(s):
            to = z_peer(s)
            send(a.at[chunk, order(*to), rows], b.at[chunk, slot, rows], 0, chunk, to)

    def arrive(stage, chunk, source, target):
        view = pltpu.make_async_remote_copy(
            src_ref=source,
            dst_ref=target,
            send_sem=send_sem.at[stage, chunk],
            recv_sem=recv_sem.at[stage, chunk],
            device_id=(slab, part),
            device_id_type=MESH,
        )
        return view

    def y_stage(chunk):
        keep(a.at[chunk, mine], b.at[chunk, slot], 0, chunk).wait()
        arrive(0, chunk, a.at[chunk, pl.ds(0, RING - 1)], b.at[chunk, pl.ds(0, RING - 1)]).wait_recv()
        size = 3 * LANES

        @pl.loop(0, GROUPS)
        def _(lo):
            peaks, weights = [], []
            for k in range(GROUPS):
                block = b[chunk, lo * GROUPS + k]
                peak = jnp.max(block, axis=1, keepdims=True)
                peaks.append(peak)
                weights.append(jnp.exp(block - peak))
            for k in range(GROUPS):
                near = [j for j in range(k - 1, k + 2) if 0 <= j < GROUPS]
                top = peaks[near[0]]
                for j in near[1:]:
                    top = jnp.maximum(top, peaks[j])
                window = jnp.concatenate([weights[j] * jnp.exp(peaks[j] - top) for j in near], axis=1)
                high, low = halves(window)
                start = (near[0] - (k - 1)) * LANES
                width = len(near) * LANES
                tall = [y_table[i * size + start:i * size + start + width, :] for i in range(2)]
                logs = jnp.log(dot(high, tall[0]) + dot(low, tall[0]) + dot(high, tall[1])) + top
                for r in range(depth):
                    for g in range(4):
                        at = pl.multiple_of((lo * depth + r) * ROWS, ROWS)
                        first = (r * 4 + g) * ROWS
                        c[chunk, k * 4 + g, pl.ds(at, ROWS), :] = logs[first:first + ROWS, :]

        rows = pl.ds(pl.multiple_of(spot * tile, tile), tile)
        keep(c.at[chunk, spot], d.at[chunk, rows], 1, chunk).start()

        @pl.loop(1, RING)
        def _(s):
            to = xy_peer(s)
            send(c.at[chunk, to], d.at[chunk, rows], 1, chunk, (to * GROUPS + lane, part))

    def z_stage(chunk):
        rows = pl.ds(pl.multiple_of(spot * tile, tile), tile)
        keep(c.at[chunk, spot], d.at[chunk, rows], 1, chunk).wait()
        arrive(1, chunk, c.at[chunk, pl.ds(0, RING - 1)], d.at[chunk, pl.ds(0, (RING - 1) * tile)]).wait_recv()
        deep = RING * tile // ROWS
        tops = jnp.max(d[chunk].reshape(deep, ROWS, LANES), axis=0)
        for x in range(0, ROWS, 2):
            top = jnp.concatenate([tops[x:x + 1, :], tops[x + 1:x + 2, :]], axis=1)
            pair = jnp.concatenate([d[chunk, pl.ds(x + i, deep, stride=ROWS), :] for i in range(2)], axis=1)
            high, low = halves(jnp.exp(pair - top))
            logs = jnp.log(dot(z_table[...], jnp.concatenate([high, low, high], axis=0))) + top
            for i in range(2):
                e[chunk, pl.ds(x + i, deep, stride=ROWS), :] = logs[:, i * LANES:(i + 1) * LANES]
        keep(e.at[chunk, rows], f.at[chunk, spot], 2, chunk).start()

        @pl.loop(1, RING)
        def _(s):
            to = xy_peer(s)
            there = pl.ds(pl.multiple_of(to * tile, tile), tile)
            send(e.at[chunk, there], f.at[chunk, spot], 2, chunk, (to * GROUPS + lane, part))

    def piece(chunk, slab_of, part_of):
        rows = tile // GROUPS
        at = pl.multiple_of((slab_of % GROUPS) * rows, rows)
        return f.at[chunk, pl.ds(part_of * 4, 4), pl.ds(at, rows)]

    def back_wait(chunk):
        rows = pl.ds(pl.multiple_of(spot * tile, tile), tile)
        keep(e.at[chunk, rows], f.at[chunk, spot], 2, chunk).wait()
        arrive(2, chunk, e.at[chunk, pl.ds(0, (RING - 1) * tile)], f.at[chunk, pl.ds(0, RING - 1)]).wait_recv()

    def back_send(source, target, stage, column):
        keep(source(slab, part), target, stage, column).start()

        @pl.loop(1, RING)
        def _(s):
            to = z_peer(s)
            send(source(*to), target, stage, column, to)

    def back_stage(chunk):
        back_wait(chunk)
        back_send(functools.partial(piece, chunk), home.at[chunk, mine], 3, chunk)

    final = CHUNKS - 1

    def row_piece(r, slab_of, part_of):
        at = pl.multiple_of((slab_of % GROUPS) * (tile // GROUPS) + r * ROWS, ROWS)
        return f.at[final, pl.ds(part_of * 4, 4), pl.ds(at, ROWS)]

    def row_place(r, which):
        return rest.at[which] if r == depth - 1 else home.at[final, which, :, pl.ds(r * ROWS, ROWS)]

    row_sems = [(3, final)] + [(4, r - 1) for r in range(1, depth)]

    edge = jnp.full((depth, own_rows, LANES), EMPTY, jnp.float32)
    cells[:, :, :LANES] = edge
    cells[:, :, LANES + length:] = edge
    loads[0].wait()
    tables[0].wait()
    for r in range(depth):
        x_row(0, r)
        if r == 0:
            meet_z()
        x_send(0, r)
    keep(a.at[0, mine], b.at[0, slot], 0, 0).start()
    for load in loads[1:2] + tables[1:]:
        load.wait()

    @pl.loop(1, CHUNKS)
    def _(chunk):
        @pl.loop(0, depth)
        def _(r):
            x_row(chunk, r)

        keep(a.at[chunk, mine], b.at[chunk, slot], 0, chunk).start()
        x_send(chunk)

    meet_xy()

    @pl.loop(0, CHUNKS)
    def _(chunk):
        y_stage(chunk)

        @pl.when(chunk > 0)
        def _():
            back_stage(chunk - 1)

        z_stage(chunk)

    back_wait(final)
    for r in range(depth):
        back_send(functools.partial(row_piece, r), row_place(r, mine), *row_sems[r])
    loads[2].wait()
    pass_on = pltpu.make_async_copy(
        outer_in.at[pl.ds(depth - 1, 1), :, pl.ds(length - step_x, step_x)], rest_outer, load_sem.at[2]
    )
    pass_on.start()
    pass_on.wait()
    some = pl.ds(0, RING - 1)

    def out_copies(rows, chunk, column):
        at = pl.ds(pl.multiple_of(chunk * step_x, step_x), step_x)
        return [
            pltpu.make_async_copy(source.at[rows, :, at], target.at[rows, :, at], out_sem.at[i, column])
            for i, (source, target) in enumerate(((dual_in, done_dual), (density_in, done_density)))
        ]

    every = pl.ds(0, depth)

    def row(chunk, r):
        def turned(k):
            rows = pl.ds(pl.multiple_of(r * ROWS, ROWS), ROWS)
            return home[chunk, 8 * k:8 * k + 8, :, rows, :].reshape(WIDE, LANES)

        finish(turned, outer_in, (chunk * step_x, step_x), r, chunk * step_x, dual_in, density_in)

    @pl.loop(0, final)
    def _(chunk):
        keep(piece(chunk, slab, part), home.at[chunk, mine], 3, chunk).wait()
        arrive(3, chunk, home.at[chunk, some], home.at[chunk, some]).wait_recv()

        @pl.loop(0, depth)
        def _(r):
            row(chunk, r)

        for copy in out_copies(every, chunk, chunk):
            copy.start()

    for r in range(depth):
        keep(row_piece(r, slab, part), row_place(r, mine), *row_sems[r]).wait()
        if r == depth - 1:
            break
        arrive(*row_sems[r], row_place(r, some), row_place(r, some)).wait_recv()
        row(final, r)
        for copy in out_copies(pl.ds(r, 1), final, final + r):
            copy.start()

    @pl.loop(0, final)
    def _(chunk):
        for copy in out_copies(every, chunk, chunk):
            copy.wait()

    for r in range(depth - 1):
        for copy in out_copies(pl.ds(r, 1), final, final + r):
            copy.wait()

    @pl.loop(0, CHUNKS)
    def _(chunk):
        flat = pl.ds(0, (RING - 1) * tile)
        arrive(0, chunk, a.at[chunk, some], b.at[chunk, some]).wait_send()
        arrive(1, chunk, c.at[chunk, some], d.at[chunk, flat]).wait_send()
        arrive(2, chunk, e.at[chunk, flat], f.at[chunk, some]).wait_send()

    @pl.loop(0, final)
    def _(chunk):
        arrive(3, chunk, home.at[chunk, some], home.at[chunk, some]).wait_send()

    for r in range(depth):
        arrive(*row_sems[r], row_place(r, some), row_place(r, some)).wait_send()
    arrive(*row_sems[-1], row_place(depth - 1, some), row_place(depth - 1, some)).wait_recv()


def local(potential, external):
    depth, own_rows, length = potential.shape
    groups = lax.axis_size("gz")
    rows = depth * ROWS
    tile = GROUPS * rows
    wide = length // CHUNKS
    anywhere = pl.BlockSpec(memory_space=pl.ANY)
    x_table = jnp.asarray(table_rows(log_kernel(4 * LANES, WIDE, RADIUS, RADIUS)))
    y_table = jnp.asarray(table_rows(log_kernel(3 * LANES, LANES, RADIUS, RADIUS)))
    z_table = jnp.asarray(table_cols(log_kernel(groups * depth, groups * depth, 0, RADIUS)))
    stack = pltpu.VMEM((CHUNKS, RING, tile, LANES), jnp.float32)
    long = pltpu.VMEM((CHUNKS, RING * tile, LANES), jnp.float32)
    field = jax.ShapeDtypeStruct(potential.shape, jnp.float32)
    held = pltpu.VMEM(potential.shape, jnp.float32)
    piece = (RING, GROUPS, ROWS, LANES)
    done_dual, done_density, rest, rest_outer = pl.pallas_call(
        chain_kernel,
        out_shape=(
            field,
            field,
            jax.ShapeDtypeStruct(piece, jnp.float32),
            jax.ShapeDtypeStruct((1, own_rows, wide), jnp.float32),
        ),
        in_specs=[pl.BlockSpec(memory_space=pltpu.HBM)] * 5,
        out_specs=(anywhere,) * 4,
        scratch_shapes=[
            pltpu.VMEM((depth, own_rows, length + 2 * LANES), jnp.float32),
            stack,
            stack,
            stack,
            long,
            long,
            stack,
            pltpu.VMEM((CHUNKS, RING, GROUPS, rows, LANES), jnp.float32),
            held,
            held,
            held,
            *[pltpu.VMEM(table.shape, table.dtype) for table in (x_table, y_table, z_table)],
            pltpu.SemaphoreType.DMA((6,)),
            pltpu.SemaphoreType.DMA((5, CHUNKS)),
            pltpu.SemaphoreType.DMA((5, CHUNKS)),
            pltpu.SemaphoreType.DMA((5, CHUNKS)),
            pltpu.SemaphoreType.DMA((2, CHUNKS - 1 + depth)),
            pltpu.SemaphoreType.REGULAR,
            pltpu.SemaphoreType.REGULAR,
        ],
        compiler_params=pltpu.CompilerParams(collective_id=0, has_side_effects=True, vmem_limit_bytes=44 << 20),
        name="along_xyz",
    )(*[pltpu.with_memory_space_constraint(v, pltpu.HBM) for v in (potential, external, x_table, y_table, z_table)])
    late = pltpu.VMEM((1, own_rows, wide), jnp.float32)
    return pl.pallas_call(
        end_kernel,
        out_shape=(field, field),
        in_specs=[anywhere] * 4,
        out_specs=(anywhere, anywhere),
        scratch_shapes=[pltpu.VMEM(piece, jnp.float32), late, late, late, pltpu.SemaphoreType.DMA((8,))],
        compiler_params=pltpu.CompilerParams(vmem_limit_bytes=16 << 20),
        name="proximal",
    )(done_dual, done_density, rest, rest_outer)


def solution(mesh):
    return jax.shard_map(
        local,
        mesh=mesh,
        in_specs=(P("gz", "gy", None), P("gz", "gy", None)),
        out_specs=(P("gz", "gy", None), P("gz", "gy", None)),
        check_vma=False,
    )
```
